32 devices in a mesh: space: 8 (over z, y), fsdp: 4 (over x, core).
Axes of the slice: x: 2, y: 2, z: 4, core: 2. Of those that a mesh axis runs over, the one named last changes fastest.
Arguments:
- features: bfloat16 [8, 4, 384, 384], P('space', 'fsdp'), may hold values from -60 to 60
- channel_gain: float32 [384], replicated, may hold values from 0.5 to 2
- conv_weight: bfloat16 [27, 384, 384], P(None, 'space', 'fsdp'), may hold values from -0.0625 to 0.0625
- kernel_map: int32 [8, 4, 27, 384], P('space', 'fsdp'), may hold values from 0 to 1536, as said below
- counts: int32 [8, 4, 3], P('space', 'fsdp'), may hold values from 1 to 128, as said below
- halo_list: int32 [8, 4, 1], P('space', 'fsdp'), may hold values from 0 to 2
- skip_dest: int32 [8, 4, 384, 1], P('space', 'fsdp'), may hold values from 0 to 7; in each aligned block of 384 rows (0 to 383, 384 to 767, ..., all dimensions but the last counted through in order) at most 96 rows name the same one
- out_grad: bfloat16 [8, 4, 384, 384], P('space', 'fsdp'), may hold values from -6 to 6
Outputs:
- section_out: bfloat16 [8, 4, 384, 384], P('space', 'fsdp')
- feature_grad: bfloat16 [8, 4, 384, 384], P('space', 'fsdp')
- skip_recv: bfloat16 [8, 4, 8, 96, 384], P('space', 'fsdp')
The draws below stay inside these ranges and needn't reach their ends.
Inputs may be any that keep to these rules, and one draw needn't show every extreme that they name: kernel_map[s, f, k, i] is a row of the table lookup[s, f]; the value 1536 means that offset k has no neighbour; at the middle offset every row names itself. `counts`: every device has a block with all 128 slots active. `skip_dest`: at most 96 rows of one device name one owner, and in every draw some device sends exactly 96 rows to some owner.
All inputs are finite; a program needn't handle non-finite values.
Results may differ from the reference program's by a relative error of at most 0.0045.
Values may be sent and summed in bfloat16 or wider, within the bound.
A program may use at most 64 MiB of HBM per device.

```python
import math
import jax
import jax.numpy as jnp
import numpy as np
from jax import lax

C = 384
BLK = 128
KOFF = 27
HB = 1
NB = 3
ROWS = 1536
MOST = 96
N_SPACE = 8
N_FSDP = 4


def draw_features(key, part):
    key_base, key_rows, key_cols = jax.random.split(key, 3)
    array_shape = (N_SPACE, N_FSDP, NB * BLK, C)
    row_scale = jnp.exp(jax.random.uniform(key_rows, (N_SPACE, N_FSDP, NB * BLK, 1), jnp.float32, -1.15, 1.15))
    col_scale = jnp.exp(jax.random.uniform(key_cols, (C,), jnp.float32, -1.15, 1.15))
    base_values = jax.random.truncated_normal(key_base, -5.0, 5.0, array_shape, jnp.float32)
    return (base_values * row_scale * col_scale).astype(jnp.bfloat16)


def draw_kernel_map(key, part):
    key_block, key_slot, key_gap = jax.random.split(key, 3)
    array_shape = (N_SPACE, N_FSDP, KOFF, NB * BLK)
    blocks = jax.random.randint(key_block, array_shape, 0, NB + 9 * HB)
    slot_pick = jax.random.randint(key_slot, array_shape, 0, BLK)
    absent = jax.random.randint(key_gap, array_shape, 0, 4) == 0
    picked = jnp.where(absent, ROWS, blocks * BLK + slot_pick)
    offsets = lax.broadcasted_iota(jnp.int32, array_shape, 2)
    rows_self = lax.broadcasted_iota(jnp.int32, array_shape, 3)
    return jnp.where(offsets == KOFF // 2, rows_self, picked).astype(jnp.int32)


def draw_counts(key, part):
    key_count, key_full = jax.random.split(key)
    array_shape = (N_SPACE, N_FSDP, NB)
    drawn_counts = jax.random.randint(key_count, array_shape, 1, BLK + 1)
    full_block = jax.random.randint(key_full, (N_SPACE, N_FSDP, 1), 0, NB)
    block_ids = lax.broadcasted_iota(jnp.int32, array_shape, 2)
    return jnp.where(block_ids == full_block, BLK, drawn_counts).astype(jnp.int32)


def touch_ends(entries, own_key, least, high):
    longest = entries.shape.index(max(entries.shape))
    spots = []
    for shift in (0, 1):
        where = [jax.random.randint(jax.random.fold_in(own_key, axis), (), 0, length) for axis, length in enumerate(entries.shape)]
        where[longest] = (where[longest] + shift) % entries.shape[longest]
        spots.append(tuple(where))
    return entries.at[spots[0]].set(least).at[spots[1]].set(high)


def levels(key, dims, shards, smallest, top_value):
    factor_of = 1.0
    for axis_at, shards_of in shards:
        steps = jax.random.uniform(jax.random.fold_in(jax.random.fold_in(key, 6), axis_at), (shards_of,), jnp.float32, smallest / len(shards), top_value / len(shards))
        factor_of = factor_of * jnp.repeat(jnp.exp(steps), dims[axis_at] // shards_of).reshape((-1,) + (1,) * (len(dims) - 1 - axis_at))
    return factor_of


def shared_out(key, own, number, rows, number_of, top, bound, slope):
    sequence = jax.random.permutation(key, number_of)
    crowded, ordinary = portions_of(number_of, rows * top, bound, slope, True), portions_of(number_of, rows * top, bound, slope, False)
    places = jnp.arange(number_of)

    def named(sizes, offset_by):
        used = int((sizes > 0).sum())
        fixed = max(1, used // 4)
        passed = fixed + (places - fixed + offset_by * (used - fixed)) % max(1, number_of - fixed)
        return jnp.zeros((number_of,), jnp.int32).at[sequence[jnp.where(places < fixed, places, passed)]].set(jnp.asarray(sizes, jnp.int32))

    sizes = jnp.where(number % 4 == 0, named(crowded, number // 4), named(ordinary, number - number // 4 - 1))
    mixed = jax.random.permutation(jax.random.fold_in(own, 3), number_of)
    giver, receiver = mixed[0:number_of // 2 * 2:2], mixed[1:number_of // 2 * 2:2]
    margin = jnp.minimum(sizes[giver] - 1, bound - sizes[receiver]) // 2
    margin = jnp.where((giver == sequence[0]) | (receiver == sequence[0]) | (sizes[receiver] == 0), 0, jnp.maximum(margin, 0))
    passed = jax.random.randint(jax.random.fold_in(own, 4), (number_of // 2,), 0, 1 << 20) % (margin + 1)
    sizes = sizes.at[giver].add(-passed).at[receiver].add(passed)
    items = jnp.searchsorted(jnp.cumsum(sizes), jnp.arange(rows * top), side="right").astype(jnp.int32)
    table = items.reshape(top, rows).T
    table = table[jax.random.permutation(jax.random.fold_in(own, 1), rows)]
    offset_by = jax.random.randint(jax.random.fold_in(own, 2), (rows, 1), 0, top)
    return jnp.take_along_axis(table, (jnp.arange(top)[None, :] + offset_by) % top, axis=1)


def portions_of(number_of, total, reach, lean, full):
    portions = [(1 << 20) // math.isqrt(grade ** lean) + 1 for grade in range(1, number_of + 1)]
    largest = reach if full else min(reach, max(-(-total // number_of), total * portions[0] // sum(portions)))
    least = 1 if total - largest >= number_of - 1 else 0
    holding, rest = [largest] + [least] * (number_of - 1), total - largest - least * (number_of - 1)
    while rest > 0:
        candidates = [i for i in range(1, number_of) if holding[i] < largest] or [i for i in range(1, number_of) if holding[i] < reach]
        pool, budget = sum([portions[i] for i in candidates]), rest
        for i in candidates:
            more = min(reach - holding[i], max(1, budget * portions[i] // pool), rest)
            holding[i] = holding[i] + more
            rest = rest - more
    return np.array(holding)


def scatter_about(key, shape, deviation, most, cuts=(), kind=jnp.bfloat16):
    gain = levels(key, shape, cuts, -0.22, 0.18) if cuts else 1.0
    values = jax.random.normal(key, shape, jnp.float32) * deviation * gain
    return jnp.minimum(jnp.maximum(values, -most), most).astype(kind)


def setup_inputs(seed: int = 0) -> dict:
    streams_of = jax.random.split(jax.random.key(seed), 9)
    features = draw_features(jax.random.fold_in(streams_of[8], 71), 0)
    channel_gain = jnp.clip(jnp.exp(jax.random.uniform(streams_of[1], (C,), jnp.float32, math.log(0.5), math.log(2.0))), 0.5, 2.0)
    conv_weight = scatter_about(streams_of[2], (KOFF, C, C), (KOFF * C) ** -0.5, 0.0625, ((1, 8), (2, 4)))
    kernel_map = draw_kernel_map(jax.random.fold_in(streams_of[8], 71), 0)
    counts = draw_counts(jax.random.fold_in(streams_of[8], 71), 0)
    halo_list = touch_ends(jax.random.randint(streams_of[5], (N_SPACE, N_FSDP, HB), 0, NB), jax.random.fold_in(streams_of[5], 1), 0, NB - 1).astype(jnp.int32)
    skip_dest_keys = jax.random.split(jax.random.fold_in(streams_of[6], 1), N_SPACE * N_FSDP * (NB * BLK) // (NB * BLK))
    skip_dest_turns = jax.random.permutation(jax.random.fold_in(streams_of[6], 3), N_SPACE * N_FSDP * (NB * BLK) // (NB * BLK))
    skip_dest = jax.vmap(lambda own, number: shared_out(jax.random.fold_in(streams_of[6], 2), own, number, NB * BLK, N_SPACE, 1, MOST, 2))(skip_dest_keys, skip_dest_turns).reshape((N_SPACE, N_FSDP, NB * BLK, 1))
    out_grad = scatter_about(streams_of[7], (N_SPACE, N_FSDP, NB * BLK, C), 1.0, 6.0, ((0, 8), (1, 4)))
    return {"features": features, "channel_gain": channel_gain, "conv_weight": conv_weight, "kernel_map": kernel_map, "counts": counts, "halo_list": halo_list, "skip_dest": skip_dest, "out_grad": out_grad}


NORM_EPS = 1e-06

def forward_parts(features, channel_gain, counts):
    rowcount = features.shape[2]
    slot_ids = jnp.arange(rowcount, dtype=jnp.int32)
    limits = jnp.repeat(counts, BLK, axis=2)
    active = ((slot_ids % BLK)[None, None, :] < limits).astype(jnp.float32)[..., None]
    masked = features * active.astype(jnp.bfloat16)
    masked_f = masked.astype(jnp.float32)
    rscale = lax.rsqrt(lax.optimization_barrier(jnp.mean(masked_f * masked_f, axis=-1, keepdims=True)) + NORM_EPS)
    normed = masked_f * rscale
    pre_act = normed * channel_gain
    act = jax.nn.silu(pre_act).astype(jnp.bfloat16)
    return (slot_ids, active, masked_f, rscale, normed, pre_act, act)

def reference(features, channel_gain, conv_weight, kernel_map, counts, halo_list, skip_dest, out_grad):
    space_size = N_SPACE
    fsdp_size = N_FSDP
    rowcount = NB * BLK
    slot_ids, active, masked_f, rscale, normed, pre_act, act = forward_parts(features, channel_gain, counts)
    blocked = act.reshape(space_size, fsdp_size, NB, BLK, C)
    shared = jax.vmap(jax.vmap(lambda blocks_here, chosen: blocks_here[chosen]))(blocked, halo_list)
    padded = jnp.pad(shared, ((1, 1), (1, 1), (0, 0), (0, 0), (0, 0)))
    beside_all = jnp.stack([padded[1 + shift_s:1 + shift_s + space_size, 1 + shift_f:1 + shift_f + fsdp_size] for shift_s in (-1, 0, 1) for shift_f in (-1, 0, 1)], axis=2)
    lookup = jnp.concatenate([act, beside_all.reshape(space_size, fsdp_size, 9 * HB * BLK, C), jnp.zeros((space_size, fsdp_size, 1, C), jnp.bfloat16)], axis=2)
    row_grad = out_grad * active.astype(jnp.bfloat16)

    def device_pass(packed):
        table_here, map_here, grad_here = packed

        def offset_step(state, inputs_k):
            running, table_grad = state
            weight_k, map_k = inputs_k
            running = running + jnp.dot(table_here[map_k], weight_k, preferred_element_type=jnp.float32)
            backward = jnp.dot(grad_here, weight_k.T, preferred_element_type=jnp.float32)
            table_grad = table_grad.at[map_k].add(backward)
            return ((running, table_grad), None)
        start = (jnp.zeros((rowcount, C), jnp.float32), jnp.zeros((ROWS + 1, C), jnp.float32))
        (running, table_grad), _ = lax.scan(offset_step, start, (conv_weight, map_here))
        return (running, table_grad[:ROWS])
    conv_sum, lookup_grad = lax.map(device_pass, (lookup.reshape(space_size * fsdp_size, ROWS + 1, C), kernel_map.reshape(space_size * fsdp_size, KOFF, rowcount), row_grad.reshape(space_size * fsdp_size, rowcount, C)))
    conv_sum = conv_sum.reshape(space_size, fsdp_size, rowcount, C)
    section_out = ((masked_f + conv_sum) * active).astype(jnp.bfloat16)
    owners = skip_dest[..., 0]
    earlier = (owners[..., None, :] == owners[..., :, None]) & (slot_ids[None, :] < slot_ids[:, None])
    placing = lax.optimization_barrier(jnp.sum(earlier.astype(jnp.int32), axis=-1))
    target = owners * MOST + placing

    def place_rows(rows_here, target_here):
        return jnp.zeros((space_size * MOST, C), jnp.bfloat16).at[target_here].set(rows_here)
    outbox = jax.vmap(jax.vmap(place_rows))(section_out, target)
    skip_recv = jnp.transpose(outbox.reshape(space_size, fsdp_size, space_size, MOST, C), (2, 1, 0, 3, 4))
    lookup_grad = lookup_grad.reshape(space_size, fsdp_size, ROWS, C)
    halo_grad = lookup_grad[:, :, rowcount:].reshape(space_size, fsdp_size, 3, 3, HB, BLK, C)
    halo_pad = jnp.pad(halo_grad, ((1, 1), (1, 1), (0, 0), (0, 0), (0, 0), (0, 0), (0, 0)))
    returned = jnp.zeros((space_size, fsdp_size, HB, BLK, C), jnp.float32)
    for shift_s in (-1, 0, 1):
        for shift_f in (-1, 0, 1):
            returned = returned + halo_pad[1 + shift_s:1 + shift_s + space_size, 1 + shift_f:1 + shift_f + fsdp_size, 1 - shift_s, 1 - shift_f]
    own_grad = lookup_grad[:, :, :rowcount].reshape(space_size, fsdp_size, NB, BLK, C)
    act_grad = jax.vmap(jax.vmap(lambda grad_here, chosen, extra: grad_here.at[chosen].add(extra)))(own_grad, halo_list, returned)
    act_grad = act_grad.reshape(space_size, fsdp_size, rowcount, C)
    sigmoid_pre = jax.nn.sigmoid(pre_act)
    pre_grad = act_grad * sigmoid_pre * (1.0 + pre_act * (1.0 - sigmoid_pre))
    normed_grad = pre_grad * channel_gain
    masked_grad = rscale * (normed_grad - normed * lax.optimization_barrier(jnp.mean(normed_grad * normed, axis=-1, keepdims=True)))
    feature_grad = ((row_grad.astype(jnp.float32) + masked_grad) * active).astype(jnp.bfloat16)
    return (section_out, feature_grad, skip_recv)
```

```python
import functools

import jax
import jax.numpy as jnp
from jax import lax
from jax.experimental import pallas as pl
from jax.experimental.pallas import tpu as pltpu
from jax.sharding import PartitionSpec as P

BLK = 128
KOFF = 27
HB = 1
NB = 3
ROWS = 1536


NORM_EPS = 1e-06


def padded(cells, sides, width):
    for axis, dim in sides:
        count = lax.axis_size(axis)
        ends = count - 1
        head = lax.slice_in_dim(cells, 0, width, axis=dim)
        tail = lax.slice_in_dim(cells, cells.shape[dim] - width, cells.shape[dim], axis=dim)
        cells = jnp.concatenate(
            [
                lax.ppermute(tail, axis, [(i, (i + 1) % count) for i in range(ends)]),
                cells,
                lax.ppermute(head, axis, [((i + 1) % count, i) for i in range(ends)]),
            ],
            axis=dim,
        )
    return cells


def passed_along(x, axis, by):
    count = lax.axis_size(axis)
    pairs = [(i, i + by) for i in range(count) if 0 <= i + by < count]
    return lax.ppermute(x, axis, pairs)


def shards_plain(features, channel_gain, conv_weight, kernel_map, counts, halo_list, skip_dest, out_grad):
    own_rows = features[0, 0]
    rowcount = own_rows.shape[0]
    width = own_rows.shape[1]
    slot_ids = jnp.arange(rowcount, dtype=jnp.int32)
    limits = jnp.repeat(counts[0, 0], BLK)
    active = (slot_ids % BLK < limits).astype(jnp.float32)[:, None]
    masked = own_rows * active.astype(jnp.bfloat16)
    masked_f = masked.astype(jnp.float32)
    rscale = lax.rsqrt(jnp.mean(masked_f * masked_f, axis=-1, keepdims=True) + NORM_EPS)
    normed = masked_f * rscale
    pre_act = normed * channel_gain
    act = jax.nn.silu(pre_act).astype(jnp.bfloat16)
    shared = act.reshape(NB, BLK, width)[halo_list[0, 0]]
    beside_all = padded(shared[None, None], (("space", 0), ("fsdp", 1)), 1)
    lookup = jnp.concatenate(
        [act, beside_all.reshape(9 * HB * BLK, width), jnp.zeros((1, width), jnp.bfloat16)], axis=0
    )
    row_grad = out_grad[0, 0] * active.astype(jnp.bfloat16)
    groups = KOFF // 3
    weight_groups = conv_weight.reshape(groups, 3, conv_weight.shape[1], conv_weight.shape[2])
    map_groups = kernel_map[0, 0].reshape(groups, 3, rowcount)

    def group_step(state, inputs_g):
        running, table_grad = state
        weight_piece, neighbours = inputs_g
        widened = lax.all_gather(weight_piece, "fsdp", axis=2, tiled=True)
        full_weights = lax.all_gather(widened, "space", axis=1, tiled=True)
        picked = lookup[neighbours]
        running = running + jnp.einsum(
            "kvc,kcd->vd", picked, full_weights, preferred_element_type=jnp.float32
        )
        backward = jnp.einsum(
            "vd,kcd->kvc", row_grad, full_weights, preferred_element_type=jnp.float32
        )
        table_grad = table_grad.at[neighbours.reshape(-1)].add(backward.reshape(-1, width))
        return ((running, table_grad), None)

    start = (jnp.zeros((rowcount, width), jnp.float32), jnp.zeros((ROWS + 1, width), jnp.float32))
    (conv_sum, table_grad), _ = lax.scan(group_step, start, (weight_groups, map_groups))
    section_out = ((masked_f + conv_sum) * active).astype(jnp.bfloat16)
    owners = skip_dest[0, 0, :, 0]
    earlier = (owners[None, :] == owners[:, None]) & (slot_ids[None, :] < slot_ids[:, None])
    placing = jnp.sum(earlier.astype(jnp.int32), axis=1)
    space_size = lax.axis_size("space")
    capacity = max(2, 2 * rowcount // space_size)
    outbox = (
        jnp.zeros((space_size * capacity, width), jnp.bfloat16)
        .at[owners * capacity + placing]
        .set(section_out)
    )
    received = lax.all_to_all(
        outbox.reshape(space_size, capacity, width),
        "space",
        split_axis=0,
        concat_axis=0,
        tiled=True,
    )
    halo_grad = table_grad[rowcount : rowcount + 9 * HB * BLK].reshape(3, 3, HB, BLK, width)
    middle = halo_grad[1]
    for direction in (1, -1):
        middle = middle + passed_along(
            halo_grad[1 + direction].astype(jnp.bfloat16), "space", direction
        ).astype(jnp.float32)
    returned = middle[1]
    for direction in (1, -1):
        returned = returned + passed_along(
            middle[1 + direction].astype(jnp.bfloat16), "fsdp", direction
        ).astype(jnp.float32)
    act_grad = table_grad[:rowcount].reshape(NB, BLK, width).at[halo_list[0, 0]].add(returned)
    act_grad = act_grad.reshape(rowcount, width)
    sigmoid_pre = jax.nn.sigmoid(pre_act)
    pre_grad = act_grad * sigmoid_pre * (1.0 + pre_act * (1.0 - sigmoid_pre))
    normed_grad = pre_grad * channel_gain
    masked_grad = rscale * (
        normed_grad - normed * jnp.mean(normed_grad * normed, axis=-1, keepdims=True)
    )
    feature_grad = ((row_grad.astype(jnp.float32) + masked_grad) * active).astype(jnp.bfloat16)
    return (section_out[None, None], feature_grad[None, None], received[None, None])


LANES = 128
Q = 3
MESH = pl.DeviceIdType.MESH
F32 = jnp.float32
BF16 = jnp.bfloat16


def moved(x, shift):
    shift = shift % LANES
    return x if shift == 0 else pltpu.roll(x, shift, 1)


def regroup(x, from_of, to_of, width, pieces):
    lanes = lax.broadcasted_iota(jnp.int32, (x.shape[0], LANES), 1)
    tiles = {}
    for p in range(pieces):
        r = 0
        while r < width:
            src, dst = from_of(p, r), to_of(p, r)
            span = min(width - r, LANES - src % LANES, LANES - dst % LANES)
            at = src // LANES * LANES
            value = moved(x[:, at : at + LANES], dst - src)
            low = dst % LANES
            held = tiles.get(dst // LANES, jnp.zeros_like(value))
            tiles[dst // LANES] = jnp.where((lanes >= low) & (lanes < low + span), value, held)
            r += span
    return jnp.concatenate([tiles[t] for t in range(len(tiles))], axis=1)


def norm_parts(feat, active, gain):
    masked = feat.astype(F32) * active
    rscale = lax.rsqrt(jnp.mean(masked * masked, axis=-1, keepdims=True) + NORM_EPS)
    normed = masked * rscale
    return masked, rscale, normed, normed * gain


NT = (((1,), (1,)), ((), ()))
TN = (((0,), (0,)), ((), ()))
SIDES = (0, -1, 1)


def place_of(ds, df):
    return NB + 3 * SIDES.index(df) + SIDES.index(ds)


def section_kernel(
    dims, h_ref, counts, feat_in, gain, og_in, w_in, maps_in, owners,
    sec_out, fgrad_out, recv,
    feat, og, wraw, nmap, active, tgt, wbuf, table, pb, conv, rgt, wcat, tgrad, gsend, grecv, mids, back_in,
    outbox, sec, fgrad, slope,
    wsend, wrecv, hsend, hrecv, ssend, srecv, bsend, brecv, load_sem, keep_sem, out_sem,
):
    S, F, Z, G, K4 = dims
    Y = 2
    rows, C = feat.shape
    width = C // F
    tiles = table.shape[0]
    span = tiles * BLK
    cap = recv.shape[1]
    koff = maps_in.shape[0]
    s = lax.axis_index("space")
    f = lax.axis_index("fsdp")
    z, y = s // Y, s % Y
    fx = (f + 2) % F
    fp = f + 1 - 2 * (f % 2)
    sy = s + 1 - 2 * y

    loads = [
        pltpu.make_async_copy(src, dst, load_sem.at[n])
        for n, (src, dst) in enumerate(
            [(w_in, wraw), (feat_in, feat), (maps_in, nmap.at[pl.ds(0, koff)]), (og_in, og)]
        )
    ]
    for c in loads:
        c.start()

    barrier = pltpu.get_barrier_semaphore()
    for d in range(1, S):
        pl.semaphore_signal(barrier, inc=1, device_id=((s + d) % S, f), device_id_type=MESH)
    for d in range(1, F):
        pl.semaphore_signal(barrier, inc=1, device_id=(s, (f + d) % F), device_id_type=MESH)

    def remote(src, dst, a, b, ss, ff):
        return pltpu.make_async_remote_copy(
            src_ref=src, dst_ref=dst, send_sem=a, recv_sem=b, device_id=(ss, ff), device_id_type=MESH
        )

    def passed(ref, g, i, ss, ff):
        return remote(ref, ref, wsend.at[g, i], wrecv.at[g, i], ss, ff)

    def first(g, d):
        return passed(wbuf.at[g, f, :, z, y], g, d - 1, ((z + d) % Z) * Y + y, f)

    B0 = Z - 1
    low, high = pl.ds(0, Z // 2), pl.ds(Z // 2, Z - Z // 2)

    def second(g):
        return [
            passed(wbuf.at[g, f, :, low, y], g, B0, sy, f),
            passed(wbuf.at[g, f, :, high, y], g, B0 + 1, s, fx),
        ]

    def third(g):
        return [
            passed(wbuf.at[g, f, :, low], g, B0 + 2, s, fx),
            passed(wbuf.at[g, f, :, high, y], g, B0 + 3, sy, f),
            passed(wbuf.at[g, fx, :, high, y], g, B0 + 4, sy, f),
        ]

    def fourth(g):
        return [
            passed(wbuf.at[g, f], g, B0 + 5, s, fp),
            passed(wbuf.at[g, fx], g, B0 + 6, s, fp),
        ]

    lane_w = lax.broadcasted_iota(jnp.int32, (wraw.shape[1], LANES), 1)
    piece = LANES - width
    loads[0].wait()
    for g in range(G):
        wide = []
        for j in range(K4):
            k = g * K4 + j
            if k < koff:
                v = wraw[k].astype(F32)
                wide.append(jnp.concatenate([v, jnp.zeros((v.shape[0], piece), F32)], axis=1))
            else:
                wide.append(jnp.zeros((wraw.shape[1], LANES), F32))
        for q in range(Q):
            extra = moved(wide[Q], width - q * piece)
            wbuf[g, f, q, z, y] = jnp.where(lane_w < width, wide[q], extra).astype(BF16)

    pl.semaphore_wait(barrier, S + F - 2)

    @pl.loop(0, G)
    def _(g):
        for d in range(1, Z):
            first(g, d).start()

    slot = lax.broadcasted_iota(jnp.int32, (BLK, 1), 0)
    for b in range(NB):
        active[b * BLK : (b + 1) * BLK] = jnp.where(slot < counts[b], 1.0, 0.0)
    gains = gain[...].reshape(1, C)
    loads[1].wait()
    h = h_ref[0]
    share = jnp.zeros((C, BLK), F32)
    for b in range(NB):
        r0 = b * BLK
        masked, rscale, normed, pre = norm_parts(feat[r0 : r0 + BLK], active[r0 : r0 + BLK], gains)
        sig = 1.0 / (1.0 + jnp.exp(-pre))
        slope[r0 : r0 + BLK] = sig * (1.0 + pre * (1.0 - sig)) * gains
        act = jnp.transpose(pre * sig)
        table[b] = act.astype(BF16)
        share = jnp.where(h == b, act, share)
    mine = place_of(0, 0)
    table[mine] = share.astype(BF16)

    def along(ds):
        n = SIDES.index(ds) - 1
        return remote(table.at[mine], table.at[place_of(ds, 0)], hsend.at[n], hrecv.at[n], s - ds, f)

    def aside(df):
        n = SIDES.index(df) + 1
        return remote(
            table.at[pl.ds(mine, 1)], table.at[pl.ds(place_of(0, df), 1)], hsend.at[n], hrecv.at[n], s, f - df
        )

    def corner(df):
        n = SIDES.index(df) + 3
        return remote(
            table.at[pl.ds(mine + 1, 2)], table.at[pl.ds(place_of(0, df) + 1, 2)], hsend.at[n], hrecv.at[n], s, f - df
        )

    def has_s(ds):
        return (s + ds >= 0) & (s + ds < S)

    def has_f(df):
        return (f + df >= 0) & (f + df < F)

    for d in (-1, 1):

        @pl.when(has_s(-d))
        def _():
            along(d).start()

        @pl.when(has_f(-d))
        def _():
            aside(d).start()

        @pl.when(jnp.logical_not(has_s(d)))
        def _():
            table[place_of(d, 0)] = jnp.zeros((C, BLK), BF16)

        @pl.when(jnp.logical_not(has_f(d)))
        def _():
            table[pl.ds(place_of(0, d), 3)] = jnp.zeros((3, C, BLK), BF16)

        @pl.when(jnp.logical_not(has_f(-d)))
        def _():
            grecv[SIDES.index(d) - 1] = jnp.zeros((3, C, BLK), BF16)

        @pl.when(jnp.logical_not(has_s(-d)))
        def _():
            back_in[SIDES.index(d) - 1] = jnp.zeros((C, BLK), BF16)

    loads[2].wait()
    nmap[koff:] = jnp.full((nmap.shape[0] - koff, 1, rows), span, jnp.int32)
    ids = nmap[...]
    block = ids // BLK
    moves = jnp.zeros_like(ids)
    for n in range(9):
        ds, df = n // 3 - 1, n % 3 - 1
        moves = jnp.where(block == NB + n, (place_of(ds, df) - NB - n) * BLK, moves)
    nmap[...] = ids + moves

    for d in (-1, 1):

        @pl.when(has_s(d))
        def _():
            along(d).wait_recv()

    for d in (-1, 1):

        @pl.when(has_f(-d))
        def _():
            corner(d).start()

    loads[3].wait()
    rg = og[...].astype(F32) * active[...]
    rgt[...] = jnp.transpose(
        regroup(rg, lambda p, r: p * width + r, lambda p, r: p * LANES + r, width, F)
    ).astype(BF16)
    owner_row = owners[...]
    owner_col = jnp.transpose(jnp.broadcast_to(owner_row, (8, rows)))[:, 0:1]
    row_at = lax.broadcasted_iota(jnp.int32, (rows, rows), 0)
    col_at = lax.broadcasted_iota(jnp.int32, (rows, rows), 1)
    earlier = jnp.where((owner_row == owner_col) & (row_at < col_at), 1, 0)
    tgt[...] = owner_row * cap + jnp.sum(earlier, axis=0, keepdims=True)
    conv[...] = jnp.zeros_like(conv)

    def hot(g, p0, count):
        at = lax.broadcasted_iota(jnp.int32, (count * BLK, rows), 0) + p0 * BLK
        return jnp.concatenate(
            [jnp.where(at == nmap[g * K4 + j], 1.0, 0.0).astype(BF16) for j in range(K4)], axis=1
        )

    def gather(g):
        whole = jnp.concatenate([table[p] for p in range(tiles)], axis=1)
        picked = jnp.dot(whole, hot(g, 0, tiles), preferred_element_type=F32).astype(BF16)
        for j in range(K4):
            pb[g, pl.ds(j * C, C)] = picked[:, j * rows : (j + 1) * rows]

    lane_c = lax.broadcasted_iota(jnp.int32, (C, LANES), 1)

    def gathered(g):
        for p in range(F):
            cols = slice(p * LANES, (p + 1) * LANES)
            last = jnp.zeros((C, LANES), F32)
            for q in range(Q):
                part = wbuf[g, p, q].reshape(C, LANES)
                wcat[q * C : (q + 1) * C, cols] = part
                part = moved(part.astype(F32), q * piece - width)
                last = jnp.where((lane_c >= q * piece) & (lane_c < (q + 1) * piece), part, last)
            wcat[Q * C :, cols] = last.astype(BF16)

    def forward(g):
        conv[...] += lax.dot_general(pb[g], wcat[...], TN, preferred_element_type=F32)

    def backward(g):
        pb[g] = jnp.dot(wcat[...], rgt[...], preferred_element_type=F32).astype(BF16)

    LAG = 2

    @pl.loop(0, G + 3 * LAG)
    def _(t):
        @pl.when(t < G)
        def _():
            for d in range(1, Z):
                first(t, d).wait_recv()
            for c in second(t):
                c.start()

        @pl.when((t >= LAG) & (t < G + LAG))
        def _():
            for c in second(t - LAG):
                c.wait_recv()
            for c in third(t - LAG):
                c.start()

        @pl.when((t >= 2 * LAG) & (t < G + 2 * LAG))
        def _():
            for c in third(t - 2 * LAG):
                c.wait_recv()
            for c in fourth(t - 2 * LAG):
                c.start()

        @pl.when(t == 0)
        def _():
            for d in (-1, 1):

                @pl.when(has_f(d))
                def _():
                    aside(d).wait_recv()
                    corner(d).wait_recv()

        @pl.when(t < G)
        def _():
            gather(t)

        done = t - 3 * LAG

        @pl.when(done >= 0)
        def _():
            for c in fourth(done):
                c.wait_recv()
            gathered(done)
            forward(done)

            @pl.when(done < G - 1)
            def _():
                backward(done)

    total = regroup(conv[...], lambda p, r: p * LANES + r, lambda p, r: p * width + r, width, F)
    out = ((feat[...].astype(F32) * active[...] + total) * active[...]).astype(BF16)
    sec[...] = out
    slots = lax.broadcasted_iota(jnp.int32, (S * cap, rows), 0)
    place = jnp.where(slots == tgt[...], 1.0, 0.0).astype(BF16)
    outbox[...] = jnp.dot(place, out, preferred_element_type=F32).astype(BF16).reshape(S, cap, C)

    def skip(d):
        o = (s + d) % S
        return remote(outbox.at[o], recv.at[s], ssend.at[d - 1], srecv.at[d - 1], o, f)

    for d in range(1, S):
        skip(d).start()
    keep = pltpu.make_async_copy(outbox.at[s], recv.at[s], keep_sem)
    keep.start()
    sec_copy = pltpu.make_async_copy(sec, sec_out, out_sem.at[0])
    sec_copy.start()
    backward(G - 1)

    half = tiles // 2

    def scatter(p0):
        tgrad[...] = jnp.zeros_like(tgrad)

        @pl.loop(0, G)
        def _(g):
            grads = jnp.concatenate([pb[g, pl.ds(j * C, C)] for j in range(K4)], axis=1)
            tgrad[...] += lax.dot_general(grads, hot(g, p0, half), NT, preferred_element_type=F32)

    def grad_aside(df):
        n = SIDES.index(df) - 1
        return remote(gsend.at[n], grecv.at[n], bsend.at[n], brecv.at[n], s, f + df)

    def grad_along(ds):
        n = SIDES.index(ds) - 1
        return remote(mids.at[n], back_in.at[n], bsend.at[n + 2], brecv.at[n + 2], s + ds, f)

    scatter(half)
    for d in (-1, 1):
        n = SIDES.index(d) - 1
        for i in range(3):
            at = (3 * n + i) * BLK
            gsend[n, i] = tgrad[:, at : at + BLK].astype(BF16)

        @pl.when(has_f(d))
        def _():
            grad_aside(d).start()

    scatter(0)
    for d in (-1, 1):

        @pl.when(has_f(-d))
        def _():
            grad_aside(d).wait_recv()

    def summed(i):
        at = (NB + i) * BLK
        return tgrad[:, at : at + BLK] + grecv[0, i].astype(F32) + grecv[1, i].astype(F32)

    for d in (-1, 1):
        n = SIDES.index(d) - 1
        mids[n] = summed(1 + n).astype(BF16)

        @pl.when(has_s(d))
        def _():
            grad_along(d).start()

    centre = summed(0)
    for d in (-1, 1):

        @pl.when(has_s(-d))
        def _():
            grad_along(d).wait_recv()

    back = centre + back_in[0].astype(F32) + back_in[1].astype(F32)
    outs = []
    for b in range(NB):
        r0 = b * BLK
        act_b = active[r0 : r0 + BLK]
        masked, rscale, normed, pre = norm_parts(feat[r0 : r0 + BLK], act_b, gains)
        ag = jnp.transpose(tgrad[:, r0 : r0 + BLK] + jnp.where(h == b, back, 0.0))
        ng = ag * slope[r0 : r0 + BLK]
        mg = rscale * (ng - normed * jnp.mean(ng * normed, axis=-1, keepdims=True))
        fgrad[r0 : r0 + BLK] = ((og[r0 : r0 + BLK].astype(F32) * act_b + mg) * act_b).astype(BF16)
        c = pltpu.make_async_copy(
            fgrad.at[pl.ds(r0, BLK)], fgrad_out.at[pl.ds(r0, BLK)], out_sem.at[1 + b]
        )
        c.start()
        outs.append(c)

    for d in range(1, S):
        skip(d).wait()
    keep.wait()
    sec_copy.wait()
    for d in (-1, 1):

        @pl.when(has_s(-d))
        def _():
            along(d).wait_send()

        @pl.when(has_f(-d))
        def _():
            aside(d).wait_send()
            corner(d).wait_send()

        @pl.when(has_f(d))
        def _():
            grad_aside(d).wait_send()

        @pl.when(has_s(d))
        def _():
            grad_along(d).wait_send()

    @pl.loop(0, G)
    def _(g):
        for d in range(1, Z):
            first(g, d).wait_send()

        for c in second(g) + third(g) + fourth(g):
            c.wait_send()

    for c in outs:
        c.wait()


def shards(mesh, features, channel_gain, conv_weight, kernel_map, counts, halo_list, skip_dest, out_grad):
    S, F = mesh.shape["space"], mesh.shape["fsdp"]
    koff, cin, width = conv_weight.shape
    rows, C = features.shape[2:]
    piece = LANES - width
    fits = F == 4 and S % 2 == 0 and cin % 16 == 0 and width == Q * piece and halo_list.shape[2] == 1
    if not (fits and rows == NB * BLK and 9 % NB == 0 and C == F * width):
        return shards_plain(
            features, channel_gain, conv_weight, kernel_map, counts, halo_list, skip_dest, out_grad
        )
    Z, K4 = S // 2, Q + 1
    G = -(-koff // K4)
    tiles = NB + 9
    cap = max(2, 2 * rows // S)
    owners = skip_dest[0, 0].reshape(1, rows)
    vm = pl.BlockSpec(memory_space=pltpu.VMEM)
    sm = pl.BlockSpec(memory_space=pltpu.SMEM)
    hbm = pl.BlockSpec(memory_space=pl.ANY)
    dma = pltpu.SemaphoreType.DMA
    sec, fgrad, recv = pl.pallas_call(
        functools.partial(section_kernel, (S, F, Z, G, K4)),
        out_shape=(
            jax.ShapeDtypeStruct((rows, C), BF16),
            jax.ShapeDtypeStruct((rows, C), BF16),
            jax.ShapeDtypeStruct((S, cap, C), BF16),
        ),
        in_specs=[sm, sm, hbm, vm, hbm, hbm, hbm, vm],
        out_specs=(hbm, hbm, hbm),
        scratch_shapes=[
            pltpu.VMEM((rows, C), BF16),
            pltpu.VMEM((rows, C), BF16),
            pltpu.VMEM((koff, cin, width), BF16),
            pltpu.VMEM((G * K4, 1, rows), jnp.int32),
            pltpu.VMEM((rows, 1), F32),
            pltpu.VMEM((1, rows), jnp.int32),
            pltpu.VMEM((G, F, Q, Z, 2, cin, LANES), BF16),
            pltpu.VMEM((tiles, C, BLK), BF16),
            pltpu.VMEM((G, K4 * C, rows), BF16),
            pltpu.VMEM((rows, F * LANES), F32),
            pltpu.VMEM((F * LANES, rows), BF16),
            pltpu.VMEM((K4 * C, F * LANES), BF16),
            pltpu.VMEM((C, tiles // 2 * BLK), F32),
            pltpu.VMEM((2, 3, C, BLK), BF16),
            pltpu.VMEM((2, 3, C, BLK), BF16),
            pltpu.VMEM((2, C, BLK), BF16),
            pltpu.VMEM((2, C, BLK), BF16),
            pltpu.VMEM((S, cap, C), BF16),
            pltpu.VMEM((rows, C), BF16),
            pltpu.VMEM((rows, C), BF16),
            pltpu.VMEM((rows, C), F32),
            dma((G, Z + 6)),
            dma((G, Z + 6)),
            dma((6,)),
            dma((6,)),
            dma((S - 1,)),
            dma((S - 1,)),
            dma((4,)),
            dma((4,)),
            dma((4,)),
            dma,
            dma((1 + NB,)),
        ],
        compiler_params=pltpu.CompilerParams(
            collective_id=0, has_side_effects=True, vmem_limit_bytes=56 * 1024 * 1024
        ),
        name="section",
    )(
        halo_list[0, 0], counts[0, 0], features[0, 0], channel_gain, out_grad[0, 0], conv_weight,
        kernel_map[0, 0][:, None], owners,
    )
    return (sec[None, None], fgrad[None, None], recv[None, None])


def solution(mesh):
    return jax.shard_map(
        functools.partial(shards, mesh),
        mesh=mesh,
        in_specs=(
            P("space", "fsdp", None, None),
            P(),
            P(None, "space", "fsdp"),
            P("space", "fsdp", None, None),
            P("space", "fsdp", None),
            P("space", "fsdp", None),
            P("space", "fsdp", None, None),
            P("space", "fsdp", None, None),
        ),
        out_specs=(
            P("space", "fsdp", None, None),
            P("space", "fsdp", None, None),
            P("space", "fsdp", None, None, None),
        ),
        check_vma=False,
    )
```

```python
import functools

import jax
import jax.numpy as jnp
from jax import lax
from jax.experimental import pallas as pl
from jax.experimental.pallas import tpu as pltpu
from jax.sharding import PartitionSpec as P

BLK = 128
KOFF = 27
HB = 1
NB = 3
ROWS = 1536


NORM_EPS = 1e-06


def padded(cells, sides, width):
    for axis, dim in sides:
        count = lax.axis_size(axis)
        ends = count - 1
        head = lax.slice_in_dim(cells, 0, width, axis=dim)
        tail = lax.slice_in_dim(cells, cells.shape[dim] - width, cells.shape[dim], axis=dim)
        cells = jnp.concatenate(
            [
                lax.ppermute(tail, axis, [(i, (i + 1) % count) for i in range(ends)]),
                cells,
                lax.ppermute(head, axis, [((i + 1) % count, i) for i in range(ends)]),
            ],
            axis=dim,
        )
    return cells


def passed_along(x, axis, by):
    count = lax.axis_size(axis)
    pairs = [(i, i + by) for i in range(count) if 0 <= i + by < count]
    return lax.ppermute(x, axis, pairs)


def shards_plain(features, channel_gain, conv_weight, kernel_map, counts, halo_list, skip_dest, out_grad):
    own_rows = features[0, 0]
    rowcount = own_rows.shape[0]
    width = own_rows.shape[1]
    slot_ids = jnp.arange(rowcount, dtype=jnp.int32)
    limits = jnp.repeat(counts[0, 0], BLK)
    active = (slot_ids % BLK < limits).astype(jnp.float32)[:, None]
    masked = own_rows * active.astype(jnp.bfloat16)
    masked_f = masked.astype(jnp.float32)
    rscale = lax.rsqrt(jnp.mean(masked_f * masked_f, axis=-1, keepdims=True) + NORM_EPS)
    normed = masked_f * rscale
    pre_act = normed * channel_gain
    act = jax.nn.silu(pre_act).astype(jnp.bfloat16)
    shared = act.reshape(NB, BLK, width)[halo_list[0, 0]]
    beside_all = padded(shared[None, None], (("space", 0), ("fsdp", 1)), 1)
    lookup = jnp.concatenate(
        [act, beside_all.reshape(9 * HB * BLK, width), jnp.zeros((1, width), jnp.bfloat16)], axis=0
    )
    row_grad = out_grad[0, 0] * active.astype(jnp.bfloat16)
    groups = KOFF // 3
    weight_groups = conv_weight.reshape(groups, 3, conv_weight.shape[1], conv_weight.shape[2])
    map_groups = kernel_map[0, 0].reshape(groups, 3, rowcount)

    def group_step(state, inputs_g):
        running, table_grad = state
        weight_piece, neighbours = inputs_g
        widened = lax.all_gather(weight_piece, "fsdp", axis=2, tiled=True)
        full_weights = lax.all_gather(widened, "space", axis=1, tiled=True)
        picked = lookup[neighbours]
        running = running + jnp.einsum(
            "kvc,kcd->vd", picked, full_weights, preferred_element_type=jnp.float32
        )
        backward = jnp.einsum(
            "vd,kcd->kvc", row_grad, full_weights, preferred_element_type=jnp.float32
        )
        table_grad = table_grad.at[neighbours.reshape(-1)].add(backward.reshape(-1, width))
        return ((running, table_grad), None)

    start = (jnp.zeros((rowcount, width), jnp.float32), jnp.zeros((ROWS + 1, width), jnp.float32))
    (conv_sum, table_grad), _ = lax.scan(group_step, start, (weight_groups, map_groups))
    section_out = ((masked_f + conv_sum) * active).astype(jnp.bfloat16)
    owners = skip_dest[0, 0, :, 0]
    earlier = (owners[None, :] == owners[:, None]) & (slot_ids[None, :] < slot_ids[:, None])
    placing = jnp.sum(earlier.astype(jnp.int32), axis=1)
    space_size = lax.axis_size("space")
    capacity = max(2, 2 * rowcount // space_size)
    outbox = (
        jnp.zeros((space_size * capacity, width), jnp.bfloat16)
        .at[owners * capacity + placing]
        .set(section_out)
    )
    received = lax.all_to_all(
        outbox.reshape(space_size, capacity, width),
        "space",
        split_axis=0,
        concat_axis=0,
        tiled=True,
    )
    halo_grad = table_grad[rowcount : rowcount + 9 * HB * BLK].reshape(3, 3, HB, BLK, width)
    middle = halo_grad[1]
    for direction in (1, -1):
        middle = middle + passed_along(
            halo_grad[1 + direction].astype(jnp.bfloat16), "space", direction
        ).astype(jnp.float32)
    returned = middle[1]
    for direction in (1, -1):
        returned = returned + passed_along(
            middle[1 + direction].astype(jnp.bfloat16), "fsdp", direction
        ).astype(jnp.float32)
    act_grad = table_grad[:rowcount].reshape(NB, BLK, width).at[halo_list[0, 0]].add(returned)
    act_grad = act_grad.reshape(rowcount, width)
    sigmoid_pre = jax.nn.sigmoid(pre_act)
    pre_grad = act_grad * sigmoid_pre * (1.0 + pre_act * (1.0 - sigmoid_pre))
    normed_grad = pre_grad * channel_gain
    masked_grad = rscale * (
        normed_grad - normed * jnp.mean(normed_grad * normed, axis=-1, keepdims=True)
    )
    feature_grad = ((row_grad.astype(jnp.float32) + masked_grad) * active).astype(jnp.bfloat16)
    return (section_out[None, None], feature_grad[None, None], received[None, None])


LANES = 128
Q = 3
MESH = pl.DeviceIdType.MESH
F32 = jnp.float32
BF16 = jnp.bfloat16


def moved(x, shift):
    shift = shift % LANES
    return x if shift == 0 else pltpu.roll(x, shift, 1)


def regroup(x, from_of, to_of, width, pieces):
    lanes = lax.broadcasted_iota(jnp.int32, (x.shape[0], LANES), 1)
    tiles = {}
    for p in range(pieces):
        r = 0
        while r < width:
            src, dst = from_of(p, r), to_of(p, r)
            span = min(width - r, LANES - src % LANES, LANES - dst % LANES)
            at = src // LANES * LANES
            value = moved(x[:, at : at + LANES], dst - src)
            low = dst % LANES
            held = tiles.get(dst // LANES, jnp.zeros_like(value))
            tiles[dst // LANES] = jnp.where((lanes >= low) & (lanes < low + span), value, held)
            r += span
    return jnp.concatenate([tiles[t] for t in range(len(tiles))], axis=1)


def norm_parts(feat, active, gain):
    masked = feat.astype(F32) * active
    rscale = lax.rsqrt(jnp.mean(masked * masked, axis=-1, keepdims=True) + NORM_EPS)
    normed = masked * rscale
    return masked, rscale, normed, normed * gain


NT = (((1,), (1,)), ((), ()))
TN = (((0,), (0,)), ((), ()))
SIDES = (0, -1, 1)


def place_of(ds, df):
    return NB + 3 * SIDES.index(df) + SIDES.index(ds)


def section_kernel(
    dims, h_ref, counts, feat_in, gain, og_in, w_in, maps_in, owners,
    sec_out, fgrad_out, recv,
    feat, og, wraw, nmap, active, tgt, wbuf, table, pb, conv, rgt, wcat, tgrad, gsend, grecv, mids, back_in,
    outbox, sec, fgrad, slope,
    wsend, wrecv, hsend, hrecv, ssend, srecv, bsend, brecv, load_sem, keep_sem, out_sem,
):
    S, F, Z, G, K4 = dims
    Y = 2
    rows, C = feat.shape
    width = C // F
    tiles = table.shape[0]
    span = tiles * BLK
    cap = recv.shape[1]
    koff = maps_in.shape[0]
    s = lax.axis_index("space")
    f = lax.axis_index("fsdp")
    z, y = s // Y, s % Y
    fx = (f + 2) % F
    fp = f + 1 - 2 * (f % 2)
    sy = s + 1 - 2 * y

    loads = [
        pltpu.make_async_copy(src, dst, load_sem.at[n])
        for n, (src, dst) in enumerate(
            [(w_in, wraw), (feat_in, feat), (maps_in, nmap.at[pl.ds(0, koff)]), (og_in, og)]
        )
    ]
    for c in loads:
        c.start()

    barrier = pltpu.get_barrier_semaphore()
    for d in range(1, S):
        pl.semaphore_signal(barrier, inc=1, device_id=((s + d) % S, f), device_id_type=MESH)
    for d in range(1, F):
        pl.semaphore_signal(barrier, inc=1, device_id=(s, (f + d) % F), device_id_type=MESH)

    def remote(src, dst, a, b, ss, ff):
        return pltpu.make_async_remote_copy(
            src_ref=src, dst_ref=dst, send_sem=a, recv_sem=b, device_id=(ss, ff), device_id_type=MESH
        )

    def passed(ref, g, i, ss, ff):
        return remote(ref, ref, wsend.at[g, i], wrecv.at[g, i], ss, ff)

    def first(g, d):
        return passed(wbuf.at[g, f, :, z, y], g, d - 1, ((z + d) % Z) * Y + y, f)

    B0 = Z - 1
    low, high = pl.ds(0, Z // 2), pl.ds(Z // 2, Z - Z // 2)

    def spread(g, zz):
        return [
            passed(wbuf.at[g, f, :, zz, y], g, B0 + zz, sy, f),
            passed(wbuf.at[g, f, :, zz, y], g, B0 + Z + zz, s, fx),
        ]

    def across(g):
        return [
            passed(wbuf.at[g, f, :, low, 1 - y], g, B0 + 2 * Z, s, fx),
            passed(wbuf.at[g, fx, :, high, y], g, B0 + 2 * Z + 1, sy, f),
        ]

    def twin(g):
        return [
            passed(wbuf.at[g, f], g, B0 + 2 * Z + 2, s, fp),
            passed(wbuf.at[g, fx], g, B0 + 2 * Z + 3, s, fp),
        ]

    lane_w = lax.broadcasted_iota(jnp.int32, (wraw.shape[1], LANES), 1)
    piece = LANES - width
    loads[0].wait()
    for g in range(G):
        wide = []
        for j in range(K4):
            k = g * K4 + j
            if k < koff:
                v = wraw[k].astype(F32)
                wide.append(jnp.concatenate([v, jnp.zeros((v.shape[0], piece), F32)], axis=1))
            else:
                wide.append(jnp.zeros((wraw.shape[1], LANES), F32))
        for q in range(Q):
            extra = moved(wide[Q], width - q * piece)
            wbuf[g, f, q, z, y] = jnp.where(lane_w < width, wide[q], extra).astype(BF16)

    pl.semaphore_wait(barrier, S + F - 2)

    LB, LC, LD, LG, LS, W = 2, 4, 5, 1, 9, 3

    def launch(g):
        for d in range(1, Z):
            first(g, d).start()
        for c in spread(g, z):
            c.start()

    launch(0)

    slot = lax.broadcasted_iota(jnp.int32, (BLK, 1), 0)
    for b in range(NB):
        active[b * BLK : (b + 1) * BLK] = jnp.where(slot < counts[b], 1.0, 0.0)
    gains = gain[...].reshape(1, C)
    loads[1].wait()
    h = h_ref[0]
    share = jnp.zeros((C, BLK), F32)
    for b in range(NB):
        r0 = b * BLK
        masked, rscale, normed, pre = norm_parts(feat[r0 : r0 + BLK], active[r0 : r0 + BLK], gains)
        sig = 1.0 / (1.0 + jnp.exp(-pre))
        slope[r0 : r0 + BLK] = sig * (1.0 + pre * (1.0 - sig)) * gains
        act = jnp.transpose(pre * sig)
        table[b] = act.astype(BF16)
        share = jnp.where(h == b, act, share)
    mine = place_of(0, 0)
    table[mine] = share.astype(BF16)

    def along(ds):
        n = SIDES.index(ds) - 1
        return remote(table.at[mine], table.at[place_of(ds, 0)], hsend.at[n], hrecv.at[n], s - ds, f)

    def aside(df):
        n = SIDES.index(df) + 1
        return remote(
            table.at[pl.ds(mine, 1)], table.at[pl.ds(place_of(0, df), 1)], hsend.at[n], hrecv.at[n], s, f - df
        )

    def corner(df):
        n = SIDES.index(df) + 3
        return remote(
            table.at[pl.ds(mine + 1, 2)], table.at[pl.ds(place_of(0, df) + 1, 2)], hsend.at[n], hrecv.at[n], s, f - df
        )

    def has_s(ds):
        return (s + ds >= 0) & (s + ds < S)

    def has_f(df):
        return (f + df >= 0) & (f + df < F)

    for d in (-1, 1):

        @pl.when(has_s(-d))
        def _():
            along(d).start()

        @pl.when(has_f(-d))
        def _():
            aside(d).start()

        @pl.when(jnp.logical_not(has_s(d)))
        def _():
            table[place_of(d, 0)] = jnp.zeros((C, BLK), BF16)

        @pl.when(jnp.logical_not(has_f(d)))
        def _():
            table[pl.ds(place_of(0, d), 3)] = jnp.zeros((3, C, BLK), BF16)

        @pl.when(jnp.logical_not(has_f(-d)))
        def _():
            grecv[SIDES.index(d) - 1] = jnp.zeros((3, C, BLK), BF16)

        @pl.when(jnp.logical_not(has_s(-d)))
        def _():
            back_in[SIDES.index(d) - 1] = jnp.zeros((C, BLK), BF16)

    for g in range(1, W):
        launch(g)

    loads[2].wait()
    nmap[koff:] = jnp.full((nmap.shape[0] - koff, 1, rows), span, jnp.int32)
    ids = nmap[...]
    block = ids // BLK
    moves = jnp.zeros_like(ids)
    for n in range(9):
        ds, df = n // 3 - 1, n % 3 - 1
        moves = jnp.where(block == NB + n, (place_of(ds, df) - NB - n) * BLK, moves)
    nmap[...] = ids + moves

    for d in (-1, 1):

        @pl.when(has_s(d))
        def _():
            along(d).wait_recv()

    for d in (-1, 1):

        @pl.when(has_f(-d))
        def _():
            corner(d).start()

    def hot(g, p0, count):
        at = lax.broadcasted_iota(jnp.int32, (count * BLK, rows), 0) + p0 * BLK
        return jnp.concatenate(
            [jnp.where(at == nmap[g * K4 + j], 1.0, 0.0).astype(BF16) for j in range(K4)], axis=1
        )

    def gather(g):
        whole = jnp.concatenate([table[p] for p in range(tiles)], axis=1)
        picked = jnp.dot(whole, hot(g, 0, tiles), preferred_element_type=F32).astype(BF16)
        for j in range(K4):
            pb[g, pl.ds(j * C, C)] = picked[:, j * rows : (j + 1) * rows]

    lane_c = lax.broadcasted_iota(jnp.int32, (C, LANES), 1)

    def gathered(g):
        for p in range(F):
            cols = slice(p * LANES, (p + 1) * LANES)
            last = jnp.zeros((C, LANES), F32)
            for q in range(Q):
                part = wbuf[g, p, q].reshape(C, LANES)
                wcat[q * C : (q + 1) * C, cols] = part
                part = moved(part.astype(F32), q * piece - width)
                last = jnp.where((lane_c >= q * piece) & (lane_c < (q + 1) * piece), part, last)
            wcat[Q * C :, cols] = last.astype(BF16)

    def forward(g):
        conv[...] += lax.dot_general(pb[g], wcat[...], TN, preferred_element_type=F32)

    def backward(g):
        pb[g] = jnp.dot(wcat[...], rgt[...], preferred_element_type=F32).astype(BF16)

    def scatter(g, p0, count):
        grads = jnp.concatenate([pb[g, pl.ds(j * C, C)] for j in range(K4)], axis=1)
        cols = slice(p0 * BLK, (p0 + count) * BLK)
        tgrad[:, cols] += lax.dot_general(grads, hot(g, p0, count), NT, preferred_element_type=F32)

    @pl.loop(0, G + LD)
    def _(t):
        @pl.when(t + W < G)
        def _():
            launch(t + W)

        @pl.when(t < G)
        def _():
            for d in range(1, Z):
                first(t, d).wait_recv()
                for c in spread(t, (z - d + Z) % Z):
                    c.start()

        @pl.when((t >= LB) & (t < G + LB))
        def _():
            g = t - LB
            for zz in range(Z // 2):
                spread(g, zz)[0].wait_recv()
            across(g)[0].start()
            for zz in range(Z // 2, Z):
                spread(g, zz)[1].wait_recv()
            across(g)[1].start()

        @pl.when((t >= LC) & (t < G + LC))
        def _():
            g = t - LC
            for zz in range(Z // 2):
                spread(g, zz)[1].wait_recv()
            for zz in range(Z // 2, Z):
                spread(g, zz)[0].wait_recv()
            for c in across(g):
                c.wait_recv()
            for c in twin(g):
                c.start()

        @pl.when(t == 0)
        def _():
            loads[3].wait()
            rg = og[...].astype(F32) * active[...]
            rgt[...] = jnp.transpose(
                regroup(rg, lambda p, r: p * width + r, lambda p, r: p * LANES + r, width, F)
            ).astype(BF16)
            owner_row = owners[...]
            owner_col = jnp.transpose(jnp.broadcast_to(owner_row, (8, rows)))[:, 0:1]
            row_at = lax.broadcasted_iota(jnp.int32, (rows, rows), 0)
            col_at = lax.broadcasted_iota(jnp.int32, (rows, rows), 1)
            earlier = jnp.where((owner_row == owner_col) & (row_at < col_at), 1, 0)
            tgt[...] = owner_row * cap + jnp.sum(earlier, axis=0, keepdims=True)
            conv[...] = jnp.zeros_like(conv)
            tgrad[...] = jnp.zeros_like(tgrad)

        @pl.when(t == LG)
        def _():
            for d in (-1, 1):

                @pl.when(has_f(d))
                def _():
                    aside(d).wait_recv()
                    corner(d).wait_recv()

        @pl.when((t >= LG) & (t < G + LG))
        def _():
            gather(t - LG)

        done = t - LD

        @pl.when(done >= 0)
        def _():
            for c in twin(done):
                c.wait_recv()
            gathered(done)
            forward(done)

            @pl.when(done < G - 1)
            def _():
                backward(done)

        @pl.when(t >= LS)
        def _():
            scatter(t - LS, 0, tiles)

    total = regroup(conv[...], lambda p, r: p * LANES + r, lambda p, r: p * width + r, width, F)
    out = ((feat[...].astype(F32) * active[...] + total) * active[...]).astype(BF16)
    sec[...] = out
    slots = lax.broadcasted_iota(jnp.int32, (S * cap, rows), 0)
    place = jnp.where(slots == tgt[...], 1.0, 0.0).astype(BF16)
    outbox[...] = jnp.dot(place, out, preferred_element_type=F32).astype(BF16).reshape(S, cap, C)

    def skip(d):
        o = (s + d) % S
        return remote(outbox.at[o], recv.at[s], ssend.at[d - 1], srecv.at[d - 1], o, f)

    for d in range(1, S):
        skip(d).start()
    keep = pltpu.make_async_copy(outbox.at[s], recv.at[s], keep_sem)
    keep.start()
    sec_copy = pltpu.make_async_copy(sec, sec_out, out_sem.at[0])
    sec_copy.start()
    backward(G - 1)

    def grad_aside(df):
        n = SIDES.index(df) - 1
        return remote(gsend.at[n], grecv.at[n], bsend.at[n], brecv.at[n], s, f + df)

    def grad_along(ds):
        n = SIDES.index(ds) - 1
        return remote(mids.at[n], back_in.at[n], bsend.at[n + 2], brecv.at[n + 2], s + ds, f)

    half = tiles // 2

    @pl.loop(G + LD - LS, G)
    def _(g):
        scatter(g, half, tiles - half)

    for d in (-1, 1):
        n = SIDES.index(d) - 1
        for i in range(3):
            at = (half + 3 * n + i) * BLK
            gsend[n, i] = tgrad[:, at : at + BLK].astype(BF16)

        @pl.when(has_f(d))
        def _():
            grad_aside(d).start()


    @pl.loop(G + LD - LS, G)
    def _(g):
        scatter(g, 0, half)

    for d in (-1, 1):

        @pl.when(has_f(-d))
        def _():
            grad_aside(d).wait_recv()

    def summed(i):
        at = (NB + i) * BLK
        return tgrad[:, at : at + BLK] + grecv[0, i].astype(F32) + grecv[1, i].astype(F32)

    for d in (-1, 1):
        n = SIDES.index(d) - 1
        mids[n] = summed(1 + n).astype(BF16)

        @pl.when(has_s(d))
        def _():
            grad_along(d).start()

    centre = summed(0)
    for d in (-1, 1):

        @pl.when(has_s(-d))
        def _():
            grad_along(d).wait_recv()

    back = centre + back_in[0].astype(F32) + back_in[1].astype(F32)
    outs = []
    for b in range(NB):
        r0 = b * BLK
        act_b = active[r0 : r0 + BLK]
        masked, rscale, normed, pre = norm_parts(feat[r0 : r0 + BLK], act_b, gains)
        ag = jnp.transpose(tgrad[:, r0 : r0 + BLK] + jnp.where(h == b, back, 0.0))
        ng = ag * slope[r0 : r0 + BLK]
        mg = rscale * (ng - normed * jnp.mean(ng * normed, axis=-1, keepdims=True))
        fgrad[r0 : r0 + BLK] = ((og[r0 : r0 + BLK].astype(F32) * act_b + mg) * act_b).astype(BF16)
        c = pltpu.make_async_copy(
            fgrad.at[pl.ds(r0, BLK)], fgrad_out.at[pl.ds(r0, BLK)], out_sem.at[1 + b]
        )
        c.start()
        outs.append(c)

    for d in range(1, S):
        skip(d).wait()
    keep.wait()
    sec_copy.wait()
    for d in (-1, 1):

        @pl.when(has_s(-d))
        def _():
            along(d).wait_send()

        @pl.when(has_f(-d))
        def _():
            aside(d).wait_send()
            corner(d).wait_send()

        @pl.when(has_f(d))
        def _():
            grad_aside(d).wait_send()

        @pl.when(has_s(d))
        def _():
            grad_along(d).wait_send()

    @pl.loop(0, G)
    def _(g):
        for d in range(1, Z):
            first(g, d).wait_send()

        for zz in range(Z):
            for c in spread(g, zz):
                c.wait_send()

        for c in across(g) + twin(g):
            c.wait_send()

    for c in outs:
        c.wait()


def shards(mesh, features, channel_gain, conv_weight, kernel_map, counts, halo_list, skip_dest, out_grad):
    S, F = mesh.shape["space"], mesh.shape["fsdp"]
    koff, cin, width = conv_weight.shape
    rows, C = features.shape[2:]
    piece = LANES - width
    fits = F == 4 and S % 2 == 0 and cin % 16 == 0 and width == Q * piece and halo_list.shape[2] == 1
    if not (fits and rows == NB * BLK and 9 % NB == 0 and C == F * width):
        return shards_plain(
            features, channel_gain, conv_weight, kernel_map, counts, halo_list, skip_dest, out_grad
        )
    Z, K4 = S // 2, Q + 1
    G = -(-koff // K4)
    tiles = NB + 9
    cap = max(2, 2 * rows // S)
    owners = skip_dest[0, 0].reshape(1, rows)
    vm = pl.BlockSpec(memory_space=pltpu.VMEM)
    sm = pl.BlockSpec(memory_space=pltpu.SMEM)
    hbm = pl.BlockSpec(memory_space=pl.ANY)
    dma = pltpu.SemaphoreType.DMA
    sec, fgrad, recv = pl.pallas_call(
        functools.partial(section_kernel, (S, F, Z, G, K4)),
        out_shape=(
            jax.ShapeDtypeStruct((rows, C), BF16),
            jax.ShapeDtypeStruct((rows, C), BF16),
            jax.ShapeDtypeStruct((S, cap, C), BF16),
        ),
        in_specs=[sm, sm, hbm, vm, hbm, hbm, hbm, vm],
        out_specs=(hbm, hbm, hbm),
        scratch_shapes=[
            pltpu.VMEM((rows, C), BF16),
            pltpu.VMEM((rows, C), BF16),
            pltpu.VMEM((koff, cin, width), BF16),
            pltpu.VMEM((G * K4, 1, rows), jnp.int32),
            pltpu.VMEM((rows, 1), F32),
            pltpu.VMEM((1, rows), jnp.int32),
            pltpu.VMEM((G, F, Q, Z, 2, cin, LANES), BF16),
            pltpu.VMEM((tiles, C, BLK), BF16),
            pltpu.VMEM((G, K4 * C, rows), BF16),
            pltpu.VMEM((rows, F * LANES), F32),
            pltpu.VMEM((F * LANES, rows), BF16),
            pltpu.VMEM((K4 * C, F * LANES), BF16),
            pltpu.VMEM((C, tiles * BLK), F32),
            pltpu.VMEM((2, 3, C, BLK), BF16),
            pltpu.VMEM((2, 3, C, BLK), BF16),
            pltpu.VMEM((2, C, BLK), BF16),
            pltpu.VMEM((2, C, BLK), BF16),
            pltpu.VMEM((S, cap, C), BF16),
            pltpu.VMEM((rows, C), BF16),
            pltpu.VMEM((rows, C), BF16),
            pltpu.VMEM((rows, C), F32),
            dma((G, 3 * Z + 3)),
            dma((G, 3 * Z + 3)),
            dma((6,)),
            dma((6,)),
            dma((S - 1,)),
            dma((S - 1,)),
            dma((4,)),
            dma((4,)),
            dma((4,)),
            dma,
            dma((1 + NB,)),
        ],
        compiler_params=pltpu.CompilerParams(
            collective_id=0, has_side_effects=True, vmem_limit_bytes=56 * 1024 * 1024
        ),
        name="section",
    )(
        halo_list[0, 0], counts[0, 0], features[0, 0], channel_gain, out_grad[0, 0], conv_weight,
        kernel_map[0, 0][:, None], owners,
    )
    return (sec[None, None], fgrad[None, None], recv[None, None])


def solution(mesh):
    return jax.shard_map(
        functools.partial(shards, mesh),
        mesh=mesh,
        in_specs=(
            P("space", "fsdp", None, None),
            P(),
            P(None, "space", "fsdp"),
            P("space", "fsdp", None, None),
            P("space", "fsdp", None),
            P("space", "fsdp", None),
            P("space", "fsdp", None, None),
            P("space", "fsdp", None, None),
        ),
        out_specs=(
            P("space", "fsdp", None, None),
            P("space", "fsdp", None, None),
            P("space", "fsdp", None, None, None),
        ),
        check_vma=False,
    )
```

```python
import functools

import jax
import jax.numpy as jnp
from jax import lax
from jax.experimental import pallas as pl
from jax.experimental.pallas import tpu as pltpu
from jax.sharding import PartitionSpec as P

BLK = 128
KOFF = 27
HB = 1
NB = 3
ROWS = 1536


NORM_EPS = 1e-06


def padded(cells, sides, width):
    for axis, dim in sides:
        count = lax.axis_size(axis)
        ends = count - 1
        head = lax.slice_in_dim(cells, 0, width, axis=dim)
        tail = lax.slice_in_dim(cells, cells.shape[dim] - width, cells.shape[dim], axis=dim)
        cells = jnp.concatenate(
            [
                lax.ppermute(tail, axis, [(i, (i + 1) % count) for i in range(ends)]),
                cells,
                lax.ppermute(head, axis, [((i + 1) % count, i) for i in range(ends)]),
            ],
            axis=dim,
        )
    return cells


def passed_along(x, axis, by):
    count = lax.axis_size(axis)
    pairs = [(i, i + by) for i in range(count) if 0 <= i + by < count]
    return lax.ppermute(x, axis, pairs)


def shards_plain(features, channel_gain, conv_weight, kernel_map, counts, halo_list, skip_dest, out_grad):
    own_rows = features[0, 0]
    rowcount = own_rows.shape[0]
    width = own_rows.shape[1]
    slot_ids = jnp.arange(rowcount, dtype=jnp.int32)
    limits = jnp.repeat(counts[0, 0], BLK)
    active = (slot_ids % BLK < limits).astype(jnp.float32)[:, None]
    masked = own_rows * active.astype(jnp.bfloat16)
    masked_f = masked.astype(jnp.float32)
    rscale = lax.rsqrt(jnp.mean(masked_f * masked_f, axis=-1, keepdims=True) + NORM_EPS)
    normed = masked_f * rscale
    pre_act = normed * channel_gain
    act = jax.nn.silu(pre_act).astype(jnp.bfloat16)
    shared = act.reshape(NB, BLK, width)[halo_list[0, 0]]
    beside_all = padded(shared[None, None], (("space", 0), ("fsdp", 1)), 1)
    lookup = jnp.concatenate(
        [act, beside_all.reshape(9 * HB * BLK, width), jnp.zeros((1, width), jnp.bfloat16)], axis=0
    )
    row_grad = out_grad[0, 0] * active.astype(jnp.bfloat16)
    groups = KOFF // 3
    weight_groups = conv_weight.reshape(groups, 3, conv_weight.shape[1], conv_weight.shape[2])
    map_groups = kernel_map[0, 0].reshape(groups, 3, rowcount)

    def group_step(state, inputs_g):
        running, table_grad = state
        weight_piece, neighbours = inputs_g
        widened = lax.all_gather(weight_piece, "fsdp", axis=2, tiled=True)
        full_weights = lax.all_gather(widened, "space", axis=1, tiled=True)
        picked = lookup[neighbours]
        running = running + jnp.einsum(
            "kvc,kcd->vd", picked, full_weights, preferred_element_type=jnp.float32
        )
        backward = jnp.einsum(
            "vd,kcd->kvc", row_grad, full_weights, preferred_element_type=jnp.float32
        )
        table_grad = table_grad.at[neighbours.reshape(-1)].add(backward.reshape(-1, width))
        return ((running, table_grad), None)

    start = (jnp.zeros((rowcount, width), jnp.float32), jnp.zeros((ROWS + 1, width), jnp.float32))
    (conv_sum, table_grad), _ = lax.scan(group_step, start, (weight_groups, map_groups))
    section_out = ((masked_f + conv_sum) * active).astype(jnp.bfloat16)
    owners = skip_dest[0, 0, :, 0]
    earlier = (owners[None, :] == owners[:, None]) & (slot_ids[None, :] < slot_ids[:, None])
    placing = jnp.sum(earlier.astype(jnp.int32), axis=1)
    space_size = lax.axis_size("space")
    capacity = max(2, 2 * rowcount // space_size)
    outbox = (
        jnp.zeros((space_size * capacity, width), jnp.bfloat16)
        .at[owners * capacity + placing]
        .set(section_out)
    )
    received = lax.all_to_all(
        outbox.reshape(space_size, capacity, width),
        "space",
        split_axis=0,
        concat_axis=0,
        tiled=True,
    )
    halo_grad = table_grad[rowcount : rowcount + 9 * HB * BLK].reshape(3, 3, HB, BLK, width)
    middle = halo_grad[1]
    for direction in (1, -1):
        middle = middle + passed_along(
            halo_grad[1 + direction].astype(jnp.bfloat16), "space", direction
        ).astype(jnp.float32)
    returned = middle[1]
    for direction in (1, -1):
        returned = returned + passed_along(
            middle[1 + direction].astype(jnp.bfloat16), "fsdp", direction
        ).astype(jnp.float32)
    act_grad = table_grad[:rowcount].reshape(NB, BLK, width).at[halo_list[0, 0]].add(returned)
    act_grad = act_grad.reshape(rowcount, width)
    sigmoid_pre = jax.nn.sigmoid(pre_act)
    pre_grad = act_grad * sigmoid_pre * (1.0 + pre_act * (1.0 - sigmoid_pre))
    normed_grad = pre_grad * channel_gain
    masked_grad = rscale * (
        normed_grad - normed * jnp.mean(normed_grad * normed, axis=-1, keepdims=True)
    )
    feature_grad = ((row_grad.astype(jnp.float32) + masked_grad) * active).astype(jnp.bfloat16)
    return (section_out[None, None], feature_grad[None, None], received[None, None])


LANES = 128
Q = 3
MESH = pl.DeviceIdType.MESH
F32 = jnp.float32
BF16 = jnp.bfloat16


def moved(x, shift):
    shift = shift % LANES
    return x if shift == 0 else pltpu.roll(x, shift, 1)


def regroup(x, from_of, to_of, width, pieces):
    lanes = lax.broadcasted_iota(jnp.int32, (x.shape[0], LANES), 1)
    tiles = {}
    for p in range(pieces):
        r = 0
        while r < width:
            src, dst = from_of(p, r), to_of(p, r)
            span = min(width - r, LANES - src % LANES, LANES - dst % LANES)
            at = src // LANES * LANES
            value = moved(x[:, at : at + LANES], dst - src)
            low = dst % LANES
            held = tiles.get(dst // LANES, jnp.zeros_like(value))
            tiles[dst // LANES] = jnp.where((lanes >= low) & (lanes < low + span), value, held)
            r += span
    return jnp.concatenate([tiles[t] for t in range(len(tiles))], axis=1)


def norm_parts(feat, active, gain):
    masked = feat.astype(F32) * active
    rscale = lax.rsqrt(jnp.mean(masked * masked, axis=-1, keepdims=True) + NORM_EPS)
    normed = masked * rscale
    return masked, rscale, normed, normed * gain


NT = (((1,), (1,)), ((), ()))
TN = (((0,), (0,)), ((), ()))
SIDES = (0, -1, 1)


def place_of(ds, df):
    return NB + 3 * SIDES.index(df) + SIDES.index(ds)


def section_kernel(
    dims, h_ref, counts, feat_in, gain, og_in, w_in, maps_in, owners,
    sec_out, fgrad_out, recv,
    feat, og, wraw, nmap, active, tgt, wbuf, table, pb, conv, rgt, wcat, tgrad, gsend, grecv, mids, back_in,
    outbox, sec, fgrad, slope,
    wsend, wrecv, hsend, hrecv, ssend, srecv, bsend, brecv, load_sem, keep_sem, out_sem,
):
    S, F, Z, G, K4 = dims
    Y = 2
    rows, C = feat.shape
    width = C // F
    tiles = table.shape[0]
    span = tiles * BLK
    cap = recv.shape[1]
    koff = maps_in.shape[0]
    s = lax.axis_index("space")
    f = lax.axis_index("fsdp")
    z, y = s // Y, s % Y
    fx = (f + 2) % F
    fp = f + 1 - 2 * (f % 2)
    sy = s + 1 - 2 * y

    loads = [
        pltpu.make_async_copy(src, dst, load_sem.at[n])
        for n, (src, dst) in enumerate(
            [(w_in, wraw), (feat_in, feat), (maps_in, nmap.at[pl.ds(0, koff)]), (og_in, og)]
        )
    ]
    for c in loads:
        c.start()

    barrier = pltpu.get_barrier_semaphore()
    for d in range(1, S):
        pl.semaphore_signal(barrier, inc=1, device_id=((s + d) % S, f), device_id_type=MESH)
    for d in range(1, F):
        pl.semaphore_signal(barrier, inc=1, device_id=(s, (f + d) % F), device_id_type=MESH)

    def remote(src, dst, a, b, ss, ff):
        return pltpu.make_async_remote_copy(
            src_ref=src, dst_ref=dst, send_sem=a, recv_sem=b, device_id=(ss, ff), device_id_type=MESH
        )

    def passed(ref, g, i, ss, ff):
        return remote(ref, ref, wsend.at[g, i], wrecv.at[g, i], ss, ff)

    def first(g, d):
        return passed(wbuf.at[g, f, :, z, y], g, d - 1, ((z + d) % Z) * Y + y, f)

    B0 = Z - 1
    low, high = pl.ds(0, Z // 2), pl.ds(Z // 2, Z - Z // 2)

    def spread(g, zz):
        return [
            passed(wbuf.at[g, f, :, zz, y], g, B0 + zz, sy, f),
            passed(wbuf.at[g, f, :, zz, y], g, B0 + Z + zz, s, fx),
        ]

    def across(g):
        return [
            passed(wbuf.at[g, f, :, low, 1 - y], g, B0 + 2 * Z, s, fx),
            passed(wbuf.at[g, fx, :, high, y], g, B0 + 2 * Z + 1, sy, f),
        ]

    def twin(g):
        return [
            passed(wbuf.at[g, f], g, B0 + 2 * Z + 2, s, fp),
            passed(wbuf.at[g, fx], g, B0 + 2 * Z + 3, s, fp),
        ]

    lane_w = lax.broadcasted_iota(jnp.int32, (wraw.shape[1], LANES), 1)
    piece = LANES - width
    loads[0].wait()

    def pack(g):
        wide = []
        for j in range(K4):
            k = g * K4 + j
            if k < koff:
                v = wraw[k].astype(F32)
                wide.append(jnp.concatenate([v, jnp.zeros((v.shape[0], piece), F32)], axis=1))
            else:
                wide.append(jnp.zeros((wraw.shape[1], LANES), F32))
        for q in range(Q):
            extra = moved(wide[Q], width - q * piece)
            wbuf[g, f, q, z, y] = jnp.where(lane_w < width, wide[q], extra).astype(BF16)

    pack(0)

    pl.semaphore_wait(barrier, S + F - 2)

    LB, LC, LD, LS, LE, W = 2, 4, 5, 6, 9, 3

    def launch(g):
        for c in spread(g, z):
            c.start()

    for d in range(1, Z):
        first(0, d).start()
    launch(0)

    slot = lax.broadcasted_iota(jnp.int32, (BLK, 1), 0)
    for b in range(NB):
        active[b * BLK : (b + 1) * BLK] = jnp.where(slot < counts[b], 1.0, 0.0)
    gains = gain[...].reshape(1, C)
    loads[1].wait()
    h = h_ref[0]
    share = jnp.zeros((C, BLK), F32)
    for b in range(NB):
        r0 = b * BLK
        masked, rscale, normed, pre = norm_parts(feat[r0 : r0 + BLK], active[r0 : r0 + BLK], gains)
        sig = 1.0 / (1.0 + jnp.exp(-pre))
        slope[r0 : r0 + BLK] = sig * (1.0 + pre * (1.0 - sig)) * gains
        act = jnp.transpose(pre * sig)
        table[b] = act.astype(BF16)
        share = jnp.where(h == b, act, share)
    mine = place_of(0, 0)
    table[mine] = share.astype(BF16)

    def along(ds):
        n = SIDES.index(ds) - 1
        return remote(table.at[mine], table.at[place_of(ds, 0)], hsend.at[n], hrecv.at[n], s - ds, f)

    def aside(df):
        n = SIDES.index(df) + 1
        return remote(
            table.at[pl.ds(mine, 1)], table.at[pl.ds(place_of(0, df), 1)], hsend.at[n], hrecv.at[n], s, f - df
        )

    def corner(df):
        n = SIDES.index(df) + 3
        return remote(
            table.at[pl.ds(mine + 1, 2)], table.at[pl.ds(place_of(0, df) + 1, 2)], hsend.at[n], hrecv.at[n], s, f - df
        )

    def has_s(ds):
        return (s + ds >= 0) & (s + ds < S)

    def has_f(df):
        return (f + df >= 0) & (f + df < F)

    for d in (-1, 1):

        @pl.when(has_s(-d))
        def _():
            along(d).start()

        @pl.when(has_f(-d))
        def _():
            aside(d).start()

        @pl.when(jnp.logical_not(has_s(d)))
        def _():
            table[place_of(d, 0)] = jnp.zeros((C, BLK), BF16)

        @pl.when(jnp.logical_not(has_f(d)))
        def _():
            table[pl.ds(place_of(0, d), 3)] = jnp.zeros((3, C, BLK), BF16)

        @pl.when(jnp.logical_not(has_f(-d)))
        def _():
            grecv[SIDES.index(d) - 1] = jnp.zeros((3, C, BLK), BF16)

        @pl.when(jnp.logical_not(has_s(-d)))
        def _():
            back_in[SIDES.index(d) - 1] = jnp.zeros((C, BLK), BF16)

    for g in range(1, G):
        pack(g)
        for d in range(1, Z):
            first(g, d).start()

    for g in range(1, W):
        launch(g)

    loads[2].wait()
    nmap[koff:] = jnp.full((nmap.shape[0] - koff, 1, rows), span, jnp.int32)
    ids = nmap[...]
    block = ids // BLK
    moves = jnp.zeros_like(ids)
    for n in range(9):
        ds, df = n // 3 - 1, n % 3 - 1
        moves = jnp.where(block == NB + n, (place_of(ds, df) - NB - n) * BLK, moves)
    nmap[...] = ids + moves

    for d in (-1, 1):

        @pl.when(has_s(d))
        def _():
            along(d).wait_recv()

    for d in (-1, 1):

        @pl.when(has_f(-d))
        def _():
            corner(d).start()

    def hot(g, p0, count):
        at = lax.broadcasted_iota(jnp.int32, (count * BLK, rows), 0) + p0 * BLK
        return jnp.concatenate(
            [jnp.where(at == nmap[g * K4 + j], 1.0, 0.0).astype(BF16) for j in range(K4)], axis=1
        )

    def gather(g):
        whole = jnp.concatenate([table[p] for p in range(tiles)], axis=1)
        picked = jnp.dot(whole, hot(g, 0, tiles), preferred_element_type=F32).astype(BF16)
        for j in range(K4):
            pb[g, pl.ds(j * C, C)] = picked[:, j * rows : (j + 1) * rows]

    lane_c = lax.broadcasted_iota(jnp.int32, (C, LANES), 1)

    def gathered(g):
        for p in range(F):
            cols = slice(p * LANES, (p + 1) * LANES)
            last = jnp.zeros((C, LANES), F32)
            for q in range(Q):
                part = wbuf[g, p, q].reshape(C, LANES)
                wcat[q * C : (q + 1) * C, cols] = part
                part = moved(part.astype(F32), q * piece - width)
                last = jnp.where((lane_c >= q * piece) & (lane_c < (q + 1) * piece), part, last)
            wcat[Q * C :, cols] = last.astype(BF16)

    def forward(g):
        conv[...] += lax.dot_general(pb[g], wcat[...], TN, preferred_element_type=F32)

    def backward(g):
        pb[g] = jnp.dot(wcat[...], rgt[...], preferred_element_type=F32).astype(BF16)

    def scatter(g, p0, count):
        grads = jnp.concatenate([pb[g, pl.ds(j * C, C)] for j in range(K4)], axis=1)
        cols = slice(p0 * BLK, (p0 + count) * BLK)
        tgrad[:, cols] += lax.dot_general(grads, hot(g, p0, count), NT, preferred_element_type=F32)

    @pl.loop(0, G + LD)
    def _(t):
        @pl.when(t + W < G)
        def _():
            launch(t + W)

        @pl.when(t < G)
        def _():
            for d in range(1, Z):
                first(t, d).wait_recv()
                for c in spread(t, (z - d + Z) % Z):
                    c.start()

        @pl.when((t >= LB) & (t < G + LB))
        def _():
            g = t - LB
            for zz in range(Z // 2):
                spread(g, zz)[0].wait_recv()
            across(g)[0].start()
            for zz in range(Z // 2, Z):
                spread(g, zz)[1].wait_recv()
            across(g)[1].start()

        @pl.when((t >= LC) & (t < G + LC))
        def _():
            g = t - LC
            for zz in range(Z // 2, Z):
                spread(g, zz)[0].wait_recv()
            twin(g)[0].start()
            for zz in range(Z // 2):
                spread(g, zz)[1].wait_recv()
            for c in across(g):
                c.wait_recv()
            twin(g)[1].start()

        @pl.when(t == 0)
        def _():
            loads[3].wait()
            rg = og[...].astype(F32) * active[...]
            rgt[...] = jnp.transpose(
                regroup(rg, lambda p, r: p * width + r, lambda p, r: p * LANES + r, width, F)
            ).astype(BF16)
            owner_row = owners[...]
            owner_col = jnp.transpose(jnp.broadcast_to(owner_row, (8, rows)))[:, 0:1]
            row_at = lax.broadcasted_iota(jnp.int32, (rows, rows), 0)
            col_at = lax.broadcasted_iota(jnp.int32, (rows, rows), 1)
            earlier = jnp.where((owner_row == owner_col) & (row_at < col_at), 1, 0)
            tgt[...] = owner_row * cap + jnp.sum(earlier, axis=0, keepdims=True)
            conv[...] = jnp.zeros_like(conv)
            tgrad[...] = jnp.zeros_like(tgrad)

        @pl.when(t == 1)
        def _():
            for d in (-1, 1):

                @pl.when(has_f(d))
                def _():
                    aside(d).wait_recv()
                    corner(d).wait_recv()

        @pl.loop(jnp.clip(2 * t - 3, 0, G), jnp.clip(2 * t - 1, 0, G))
        def _(g):
            gather(g)

        done = t - LD

        @pl.when(done >= 0)
        def _():
            for c in twin(done):
                c.wait_recv()
            gathered(done)
            forward(done)

            @pl.when(done < G - 1)
            def _():
                backward(done)

        @pl.when((t >= LS) & (t < LE))
        def _():
            scatter(t - LS, 0, tiles)

    total = regroup(conv[...], lambda p, r: p * LANES + r, lambda p, r: p * width + r, width, F)
    out = ((feat[...].astype(F32) * active[...] + total) * active[...]).astype(BF16)
    sec[...] = out
    far = S // 2

    def skip(d):
        o = (s + d) % S
        return remote(outbox.at[o], recv.at[s], ssend.at[d - 1], srecv.at[d - 1], o, f)

    def boxes(o0):
        slots = lax.broadcasted_iota(jnp.int32, (far * cap, rows), 0) + o0 * cap
        place = jnp.where(slots == tgt[...], 1.0, 0.0).astype(BF16)
        outbox[pl.ds(o0, far)] = jnp.dot(place, out, preferred_element_type=F32).astype(BF16).reshape(far, cap, C)

    half_s = s // far
    boxes((1 - half_s) * far)
    for d in sorted(range(1, S), key=lambda d: abs(d - far)):

        @pl.when((s + d) % S // far != half_s)
        def _():
            skip(d).start()

    boxes(half_s * far)
    for d in range(1, S):

        @pl.when((s + d) % S // far == half_s)
        def _():
            skip(d).start()

    keep = pltpu.make_async_copy(outbox.at[s], recv.at[s], keep_sem)
    keep.start()
    sec_copy = pltpu.make_async_copy(sec, sec_out, out_sem.at[0])
    sec_copy.start()
    backward(G - 1)

    def grad_aside(df):
        n = SIDES.index(df) - 1
        return remote(gsend.at[n], grecv.at[n], bsend.at[n], brecv.at[n], s, f + df)

    def grad_along(ds):
        n = SIDES.index(ds) - 1
        return remote(mids.at[n], back_in.at[n], bsend.at[n + 2], brecv.at[n + 2], s + ds, f)

    half = tiles // 2

    @pl.loop(LE - LS, G)
    def _(g):
        scatter(g, half, tiles - half)

    for d in (-1, 1):
        n = SIDES.index(d) - 1
        for i in range(3):
            at = (half + 3 * n + i) * BLK
            gsend[n, i] = tgrad[:, at : at + BLK].astype(BF16)

        @pl.when(has_f(d))
        def _():
            grad_aside(d).start()


    @pl.loop(LE - LS, G)
    def _(g):
        scatter(g, 0, half)

    for d in (-1, 1):

        @pl.when(has_f(-d))
        def _():
            grad_aside(d).wait_recv()

    def summed(i):
        at = (NB + i) * BLK
        return tgrad[:, at : at + BLK] + grecv[0, i].astype(F32) + grecv[1, i].astype(F32)

    for d in (-1, 1):
        n = SIDES.index(d) - 1
        mids[n] = summed(1 + n).astype(BF16)

        @pl.when(has_s(d))
        def _():
            grad_along(d).start()

    centre = summed(0)
    for d in (-1, 1):

        @pl.when(has_s(-d))
        def _():
            grad_along(d).wait_recv()

    back = centre + back_in[0].astype(F32) + back_in[1].astype(F32)
    outs = []
    for b in range(NB):
        r0 = b * BLK
        act_b = active[r0 : r0 + BLK]
        masked, rscale, normed, pre = norm_parts(feat[r0 : r0 + BLK], act_b, gains)
        ag = jnp.transpose(tgrad[:, r0 : r0 + BLK] + jnp.where(h == b, back, 0.0))
        ng = ag * slope[r0 : r0 + BLK]
        mg = rscale * (ng - normed * jnp.mean(ng * normed, axis=-1, keepdims=True))
        fgrad[r0 : r0 + BLK] = ((og[r0 : r0 + BLK].astype(F32) * act_b + mg) * act_b).astype(BF16)
        c = pltpu.make_async_copy(
            fgrad.at[pl.ds(r0, BLK)], fgrad_out.at[pl.ds(r0, BLK)], out_sem.at[1 + b]
        )
        c.start()
        outs.append(c)

    for d in range(1, S):
        skip(d).wait()
    keep.wait()
    sec_copy.wait()
    for d in (-1, 1):

        @pl.when(has_s(-d))
        def _():
            along(d).wait_send()

        @pl.when(has_f(-d))
        def _():
            aside(d).wait_send()
            corner(d).wait_send()

        @pl.when(has_f(d))
        def _():
            grad_aside(d).wait_send()

        @pl.when(has_s(d))
        def _():
            grad_along(d).wait_send()

    @pl.loop(0, G)
    def _(g):
        for d in range(1, Z):
            first(g, d).wait_send()

        for zz in range(Z):
            for c in spread(g, zz):
                c.wait_send()

        for c in across(g) + twin(g):
            c.wait_send()

    for c in outs:
        c.wait()


def copy_kernel(a, b, c, x, y, w, va, vb, vc, load_sem, store_sem):
    jobs = []
    for n, (src, mid, dst) in enumerate(((c, vc, w), (a, va, x), (b, vb, y))):
        load = pltpu.make_async_copy(src, mid, load_sem.at[n])
        load.start()
        jobs.append((load, pltpu.make_async_copy(mid, dst, store_sem.at[n])))
    for load, store in jobs:
        load.wait()
        store.start()
    for load, store in jobs:
        store.wait()


def shards(mesh, features, channel_gain, conv_weight, kernel_map, counts, halo_list, skip_dest, out_grad):
    S, F = mesh.shape["space"], mesh.shape["fsdp"]
    koff, cin, width = conv_weight.shape
    rows, C = features.shape[2:]
    piece = LANES - width
    fits = F == 4 and S % 2 == 0 and cin % 16 == 0 and width == Q * piece and halo_list.shape[2] == 1
    if not (fits and rows == NB * BLK and 9 % NB == 0 and C == F * width):
        return shards_plain(
            features, channel_gain, conv_weight, kernel_map, counts, halo_list, skip_dest, out_grad
        )
    Z, K4 = S // 2, Q + 1
    G = -(-koff // K4)
    tiles = NB + 9
    cap = max(2, 2 * rows // S)
    owners = skip_dest[0, 0].reshape(1, rows)
    vm = pl.BlockSpec(memory_space=pltpu.VMEM)
    sm = pl.BlockSpec(memory_space=pltpu.SMEM)
    hbm = pl.BlockSpec(memory_space=pl.ANY)
    dma = pltpu.SemaphoreType.DMA
    sec, fgrad, recv = pl.pallas_call(
        functools.partial(section_kernel, (S, F, Z, G, K4)),
        out_shape=(
            jax.ShapeDtypeStruct((rows, C), BF16),
            jax.ShapeDtypeStruct((rows, C), BF16),
            jax.ShapeDtypeStruct((S, cap, C), BF16),
        ),
        in_specs=[sm, sm, hbm, vm, hbm, hbm, hbm, vm],
        out_specs=(hbm, hbm, hbm),
        scratch_shapes=[
            pltpu.VMEM((rows, C), BF16),
            pltpu.VMEM((rows, C), BF16),
            pltpu.VMEM((koff, cin, width), BF16),
            pltpu.VMEM((G * K4, 1, rows), jnp.int32),
            pltpu.VMEM((rows, 1), F32),
            pltpu.VMEM((1, rows), jnp.int32),
            pltpu.VMEM((G, F, Q, Z, 2, cin, LANES), BF16),
            pltpu.VMEM((tiles, C, BLK), BF16),
            pltpu.VMEM((G, K4 * C, rows), BF16),
            pltpu.VMEM((rows, F * LANES), F32),
            pltpu.VMEM((F * LANES, rows), BF16),
            pltpu.VMEM((K4 * C, F * LANES), BF16),
            pltpu.VMEM((C, tiles * BLK), F32),
            pltpu.VMEM((2, 3, C, BLK), BF16),
            pltpu.VMEM((2, 3, C, BLK), BF16),
            pltpu.VMEM((2, C, BLK), BF16),
            pltpu.VMEM((2, C, BLK), BF16),
            pltpu.VMEM((S, cap, C), BF16),
            pltpu.VMEM((rows, C), BF16),
            pltpu.VMEM((rows, C), BF16),
            pltpu.VMEM((rows, C), F32),
            dma((G, 3 * Z + 3)),
            dma((G, 3 * Z + 3)),
            dma((6,)),
            dma((6,)),
            dma((S - 1,)),
            dma((S - 1,)),
            dma((4,)),
            dma((4,)),
            dma((4,)),
            dma,
            dma((1 + NB,)),
        ],
        compiler_params=pltpu.CompilerParams(
            collective_id=0, has_side_effects=True, vmem_limit_bytes=56 * 1024 * 1024
        ),
        name="section",
    )(
        halo_list[0, 0], counts[0, 0], features[0, 0], channel_gain, out_grad[0, 0], conv_weight,
        kernel_map[0, 0][:, None], owners,
    )
    whole = (sec, fgrad, recv)
    sec, fgrad, recv = pl.pallas_call(
        copy_kernel,
        out_shape=tuple(jax.ShapeDtypeStruct(v.shape, v.dtype) for v in whole),
        in_specs=[hbm] * 3,
        out_specs=(hbm,) * 3,
        scratch_shapes=[pltpu.VMEM(v.shape, v.dtype) for v in whole] + [dma((3,)), dma((3,))],
        name="deliver",
    )(*whole)
    return (sec[None, None], fgrad[None, None], recv[None, None])


def solution(mesh):
    return jax.shard_map(
        functools.partial(shards, mesh),
        mesh=mesh,
        in_specs=(
            P("space", "fsdp", None, None),
            P(),
            P(None, "space", "fsdp"),
            P("space", "fsdp", None, None),
            P("space", "fsdp", None),
            P("space", "fsdp", None),
            P("space", "fsdp", None, None),
            P("space", "fsdp", None, None),
        ),
        out_specs=(
            P("space", "fsdp", None, None),
            P("space", "fsdp", None, None),
            P("space", "fsdp", None, None, None),
        ),
        check_vma=False,
    )
```

```python
import functools

import jax
import jax.numpy as jnp
from jax import lax
from jax.experimental import pallas as pl
from jax.experimental.pallas import tpu as pltpu
from jax.sharding import PartitionSpec as P

BLK = 128
KOFF = 27
HB = 1
NB = 3
ROWS = 1536


NORM_EPS = 1e-06


def padded(cells, sides, width):
    for axis, dim in sides:
        count = lax.axis_size(axis)
        ends = count - 1
        head = lax.slice_in_dim(cells, 0, width, axis=dim)
        tail = lax.slice_in_dim(cells, cells.shape[dim] - width, cells.shape[dim], axis=dim)
        cells = jnp.concatenate(
            [
                lax.ppermute(tail, axis, [(i, (i + 1) % count) for i in range(ends)]),
                cells,
                lax.ppermute(head, axis, [((i + 1) % count, i) for i in range(ends)]),
            ],
            axis=dim,
        )
    return cells


def passed_along(x, axis, by):
    count = lax.axis_size(axis)
    pairs = [(i, i + by) for i in range(count) if 0 <= i + by < count]
    return lax.ppermute(x, axis, pairs)


def shards_plain(features, channel_gain, conv_weight, kernel_map, counts, halo_list, skip_dest, out_grad):
    own_rows = features[0, 0]
    rowcount = own_rows.shape[0]
    width = own_rows.shape[1]
    slot_ids = jnp.arange(rowcount, dtype=jnp.int32)
    limits = jnp.repeat(counts[0, 0], BLK)
    active = (slot_ids % BLK < limits).astype(jnp.float32)[:, None]
    masked = own_rows * active.astype(jnp.bfloat16)
    masked_f = masked.astype(jnp.float32)
    rscale = lax.rsqrt(jnp.mean(masked_f * masked_f, axis=-1, keepdims=True) + NORM_EPS)
    normed = masked_f * rscale
    pre_act = normed * channel_gain
    act = jax.nn.silu(pre_act).astype(jnp.bfloat16)
    shared = act.reshape(NB, BLK, width)[halo_list[0, 0]]
    beside_all = padded(shared[None, None], (("space", 0), ("fsdp", 1)), 1)
    lookup = jnp.concatenate(
        [act, beside_all.reshape(9 * HB * BLK, width), jnp.zeros((1, width), jnp.bfloat16)], axis=0
    )
    row_grad = out_grad[0, 0] * active.astype(jnp.bfloat16)
    groups = KOFF // 3
    weight_groups = conv_weight.reshape(groups, 3, conv_weight.shape[1], conv_weight.shape[2])
    map_groups = kernel_map[0, 0].reshape(groups, 3, rowcount)

    def group_step(state, inputs_g):
        running, table_grad = state
        weight_piece, neighbours = inputs_g
        widened = lax.all_gather(weight_piece, "fsdp", axis=2, tiled=True)
        full_weights = lax.all_gather(widened, "space", axis=1, tiled=True)
        picked = lookup[neighbours]
        running = running + jnp.einsum(
            "kvc,kcd->vd", picked, full_weights, preferred_element_type=jnp.float32
        )
        backward = jnp.einsum(
            "vd,kcd->kvc", row_grad, full_weights, preferred_element_type=jnp.float32
        )
        table_grad = table_grad.at[neighbours.reshape(-1)].add(backward.reshape(-1, width))
        return ((running, table_grad), None)

    start = (jnp.zeros((rowcount, width), jnp.float32), jnp.zeros((ROWS + 1, width), jnp.float32))
    (conv_sum, table_grad), _ = lax.scan(group_step, start, (weight_groups, map_groups))
    section_out = ((masked_f + conv_sum) * active).astype(jnp.bfloat16)
    owners = skip_dest[0, 0, :, 0]
    earlier = (owners[None, :] == owners[:, None]) & (slot_ids[None, :] < slot_ids[:, None])
    placing = jnp.sum(earlier.astype(jnp.int32), axis=1)
    space_size = lax.axis_size("space")
    capacity = max(2, 2 * rowcount // space_size)
    outbox = (
        jnp.zeros((space_size * capacity, width), jnp.bfloat16)
        .at[owners * capacity + placing]
        .set(section_out)
    )
    received = lax.all_to_all(
        outbox.reshape(space_size, capacity, width),
        "space",
        split_axis=0,
        concat_axis=0,
        tiled=True,
    )
    halo_grad = table_grad[rowcount : rowcount + 9 * HB * BLK].reshape(3, 3, HB, BLK, width)
    middle = halo_grad[1]
    for direction in (1, -1):
        middle = middle + passed_along(
            halo_grad[1 + direction].astype(jnp.bfloat16), "space", direction
        ).astype(jnp.float32)
    returned = middle[1]
    for direction in (1, -1):
        returned = returned + passed_along(
            middle[1 + direction].astype(jnp.bfloat16), "fsdp", direction
        ).astype(jnp.float32)
    act_grad = table_grad[:rowcount].reshape(NB, BLK, width).at[halo_list[0, 0]].add(returned)
    act_grad = act_grad.reshape(rowcount, width)
    sigmoid_pre = jax.nn.sigmoid(pre_act)
    pre_grad = act_grad * sigmoid_pre * (1.0 + pre_act * (1.0 - sigmoid_pre))
    normed_grad = pre_grad * channel_gain
    masked_grad = rscale * (
        normed_grad - normed * jnp.mean(normed_grad * normed, axis=-1, keepdims=True)
    )
    feature_grad = ((row_grad.astype(jnp.float32) + masked_grad) * active).astype(jnp.bfloat16)
    return (section_out[None, None], feature_grad[None, None], received[None, None])


LANES = 128
Q = 3
MESH = pl.DeviceIdType.MESH
F32 = jnp.float32
BF16 = jnp.bfloat16


def moved(x, shift):
    shift = shift % LANES
    return x if shift == 0 else pltpu.roll(x, shift, 1)


def regroup(x, from_of, to_of, width, pieces):
    lanes = lax.broadcasted_iota(jnp.int32, (x.shape[0], LANES), 1)
    tiles = {}
    for p in range(pieces):
        r = 0
        while r < width:
            src, dst = from_of(p, r), to_of(p, r)
            span = min(width - r, LANES - src % LANES, LANES - dst % LANES)
            at = src // LANES * LANES
            value = moved(x[:, at : at + LANES], dst - src)
            low = dst % LANES
            held = tiles.get(dst // LANES, jnp.zeros_like(value))
            tiles[dst // LANES] = jnp.where((lanes >= low) & (lanes < low + span), value, held)
            r += span
    return jnp.concatenate([tiles[t] for t in range(len(tiles))], axis=1)


def norm_parts(feat, active, gain):
    masked = feat.astype(F32) * active
    rscale = lax.rsqrt(jnp.mean(masked * masked, axis=-1, keepdims=True) + NORM_EPS)
    normed = masked * rscale
    return masked, rscale, normed, normed * gain


NT = (((1,), (1,)), ((), ()))
TN = (((0,), (0,)), ((), ()))
SIDES = (0, -1, 1)


def place_of(ds, df):
    return NB + 3 * SIDES.index(df) + SIDES.index(ds)


def section_kernel(
    dims, h_ref, counts, feat_in, gain, og_in, w_in, maps_in, owners,
    sec_out, fgrad_out, recv,
    feat, og, wraw, nmap, active, tgt, wbuf, table, pb, conv, rgt, wcat, tgrad, gsend, grecv, mids, back_in,
    outbox, sec, fgrad, slope,
    wsend, wrecv, hsend, hrecv, ssend, srecv, bsend, brecv, load_sem, keep_sem, out_sem,
):
    S, F, Z, G, K4 = dims
    Y = 2
    rows, C = feat.shape
    width = C // F
    tiles = table.shape[0]
    span = tiles * BLK
    cap = recv.shape[1]
    koff = maps_in.shape[0]
    s = lax.axis_index("space")
    f = lax.axis_index("fsdp")
    z, y = s // Y, s % Y
    fx = (f + 2) % F
    fp = f + 1 - 2 * (f % 2)
    sy = s + 1 - 2 * y

    loads = [
        pltpu.make_async_copy(src, dst, load_sem.at[n])
        for n, (src, dst) in enumerate(
            [(w_in, wraw), (feat_in, feat), (maps_in, nmap.at[pl.ds(0, koff)]), (og_in, og)]
        )
    ]
    for c in loads:
        c.start()

    barrier = pltpu.get_barrier_semaphore()
    for d in range(1, S):
        pl.semaphore_signal(barrier, inc=1, device_id=((s + d) % S, f), device_id_type=MESH)
    for d in range(1, F):
        pl.semaphore_signal(barrier, inc=1, device_id=(s, (f + d) % F), device_id_type=MESH)

    def remote(src, dst, a, b, ss, ff):
        return pltpu.make_async_remote_copy(
            src_ref=src, dst_ref=dst, send_sem=a, recv_sem=b, device_id=(ss, ff), device_id_type=MESH
        )

    def passed(ref, g, i, ss, ff):
        return remote(ref, ref, wsend.at[g, i], wrecv.at[g, i], ss, ff)

    def first(g, d):
        return passed(wbuf.at[g, f, :, z, y], g, d - 1, ((z + d) % Z) * Y + y, f)

    B0 = Z - 1
    low, high = pl.ds(0, Z // 2), pl.ds(Z // 2, Z - Z // 2)

    def spread(g, zz):
        return [
            passed(wbuf.at[g, f, :, zz, y], g, B0 + zz, sy, f),
            passed(wbuf.at[g, f, :, zz, y], g, B0 + Z + zz, s, fx),
        ]

    def across(g):
        return [
            passed(wbuf.at[g, f, :, low, 1 - y], g, B0 + 2 * Z, s, fx),
            passed(wbuf.at[g, fx, :, high, y], g, B0 + 2 * Z + 1, sy, f),
        ]

    def twin(g):
        return [
            passed(wbuf.at[g, f], g, B0 + 2 * Z + 2, s, fp),
            passed(wbuf.at[g, fx], g, B0 + 2 * Z + 3, s, fp),
        ]

    lane_w = lax.broadcasted_iota(jnp.int32, (wraw.shape[1], LANES), 1)
    piece = LANES - width
    loads[0].wait()

    def pack(g):
        wide = []
        for j in range(K4):
            k = g * K4 + j
            if k < koff:
                v = wraw[k].astype(F32)
                wide.append(jnp.concatenate([v, jnp.zeros((v.shape[0], piece), F32)], axis=1))
            else:
                wide.append(jnp.zeros((wraw.shape[1], LANES), F32))
        for q in range(Q):
            extra = moved(wide[Q], width - q * piece)
            wbuf[g, f, q, z, y] = jnp.where(lane_w < width, wide[q], extra).astype(BF16)

    pack(0)

    pl.semaphore_wait(barrier, S + F - 2)

    LB, LC, LD, LS, LE = 2, 4, 5, 6, 9

    def launch(g):
        for c in spread(g, z):
            c.start()

    for d in range(1, Z):
        first(0, d).start()
    launch(0)

    slot = lax.broadcasted_iota(jnp.int32, (BLK, 1), 0)
    for b in range(NB):
        active[b * BLK : (b + 1) * BLK] = jnp.where(slot < counts[b], 1.0, 0.0)
    gains = gain[...].reshape(1, C)
    loads[1].wait()
    h = h_ref[0]
    share = jnp.zeros((C, BLK), F32)
    for b in range(NB):
        r0 = b * BLK
        masked, rscale, normed, pre = norm_parts(feat[r0 : r0 + BLK], active[r0 : r0 + BLK], gains)
        sig = 1.0 / (1.0 + jnp.exp(-pre))
        slope[r0 : r0 + BLK] = sig * (1.0 + pre * (1.0 - sig)) * gains
        act = jnp.transpose(pre * sig)
        table[b] = act.astype(BF16)
        share = jnp.where(h == b, act, share)
    mine = place_of(0, 0)
    table[mine] = share.astype(BF16)

    def along(ds):
        n = SIDES.index(ds) - 1
        return remote(table.at[mine], table.at[place_of(ds, 0)], hsend.at[n], hrecv.at[n], s - ds, f)

    def aside(df):
        n = SIDES.index(df) + 1
        return remote(
            table.at[pl.ds(mine, 1)], table.at[pl.ds(place_of(0, df), 1)], hsend.at[n], hrecv.at[n], s, f - df
        )

    def corner(df):
        n = SIDES.index(df) + 3
        return remote(
            table.at[pl.ds(mine + 1, 2)], table.at[pl.ds(place_of(0, df) + 1, 2)], hsend.at[n], hrecv.at[n], s, f - df
        )

    def has_s(ds):
        return (s + ds >= 0) & (s + ds < S)

    def has_f(df):
        return (f + df >= 0) & (f + df < F)

    for d in (-1, 1):

        @pl.when(has_s(-d))
        def _():
            along(d).start()

        @pl.when(has_f(-d))
        def _():
            aside(d).start()

        @pl.when(jnp.logical_not(has_s(d)))
        def _():
            table[place_of(d, 0)] = jnp.zeros((C, BLK), BF16)

        @pl.when(jnp.logical_not(has_f(d)))
        def _():
            table[pl.ds(place_of(0, d), 3)] = jnp.zeros((3, C, BLK), BF16)

        @pl.when(jnp.logical_not(has_f(-d)))
        def _():
            grecv[SIDES.index(d) - 1] = jnp.zeros((3, C, BLK), BF16)

        @pl.when(jnp.logical_not(has_s(-d)))
        def _():
            back_in[SIDES.index(d) - 1] = jnp.zeros((C, BLK), BF16)

    for g in range(1, G):
        pack(g)
        for d in range(1, Z):
            first(g, d).start()

    for g in range(1, G):
        launch(g)

    loads[2].wait()
    nmap[koff:] = jnp.full((nmap.shape[0] - koff, 1, rows), span, jnp.int32)
    ids = nmap[...]
    block = ids // BLK
    moves = jnp.zeros_like(ids)
    for n in range(9):
        ds, df = n // 3 - 1, n % 3 - 1
        moves = jnp.where(block == NB + n, (place_of(ds, df) - NB - n) * BLK, moves)
    nmap[...] = ids + moves

    for d in (-1, 1):

        @pl.when(has_s(d))
        def _():
            along(d).wait_recv()

    for d in (-1, 1):

        @pl.when(has_f(-d))
        def _():
            corner(d).start()

    def hot(g, p0, count):
        at = lax.broadcasted_iota(jnp.int32, (count * BLK, rows), 0) + p0 * BLK
        return jnp.concatenate(
            [jnp.where(at == nmap[g * K4 + j], 1.0, 0.0).astype(BF16) for j in range(K4)], axis=1
        )

    def gather(g):
        whole = jnp.concatenate([table[p] for p in range(tiles)], axis=1)
        picked = jnp.dot(whole, hot(g, 0, tiles), preferred_element_type=F32).astype(BF16)
        for j in range(K4):
            pb[g, pl.ds(j * C, C)] = picked[:, j * rows : (j + 1) * rows]

    lane_c = lax.broadcasted_iota(jnp.int32, (C, LANES), 1)

    def gathered(g):
        for p in range(F):
            cols = slice(p * LANES, (p + 1) * LANES)
            last = jnp.zeros((C, LANES), F32)
            for q in range(Q):
                part = wbuf[g, p, q].reshape(C, LANES)
                wcat[q * C : (q + 1) * C, cols] = part
                part = moved(part.astype(F32), q * piece - width)
                last = jnp.where((lane_c >= q * piece) & (lane_c < (q + 1) * piece), part, last)
            wcat[Q * C :, cols] = last.astype(BF16)

    def forward(g):
        conv[...] += lax.dot_general(pb[g], wcat[...], TN, preferred_element_type=F32)

    def backward(g):
        grads = lax.dot_general(rgt[...], wcat[...], NT, preferred_element_type=F32).astype(BF16)
        for j in range(K4):
            pb[g, pl.ds(j * rows, rows)] = grads[:, j * C : (j + 1) * C]

    def scatter(g, p0, count):
        cols = slice(p0 * BLK, (p0 + count) * BLK)
        tgrad[:, cols] += lax.dot_general(pb[g], hot(g, p0, count), (((0,), (1,)), ((), ())), preferred_element_type=F32)

    @pl.loop(0, G + LD)
    def _(t):
        @pl.when(t < G)
        def _():
            for d in range(1, Z):
                first(t, d).wait_recv()
                for c in spread(t, (z - d + Z) % Z):
                    c.start()

        @pl.when((t >= LB) & (t < G + LB))
        def _():
            g = t - LB
            for zz in range(Z // 2):
                spread(g, zz)[0].wait_recv()
            across(g)[0].start()
            for zz in range(Z // 2, Z):
                spread(g, zz)[1].wait_recv()
            across(g)[1].start()

        @pl.when((t >= LC) & (t < G + LC))
        def _():
            g = t - LC
            for zz in range(Z // 2, Z):
                spread(g, zz)[0].wait_recv()
            twin(g)[0].start()
            for zz in range(Z // 2):
                spread(g, zz)[1].wait_recv()
            for c in across(g):
                c.wait_recv()
            twin(g)[1].start()

        @pl.when(t == 0)
        def _():
            loads[3].wait()
            rg = og[...].astype(F32) * active[...]
            rgt[...] = (
                regroup(rg, lambda p, r: p * width + r, lambda p, r: p * LANES + r, width, F)
            ).astype(BF16)
            owner_row = owners[...]
            owner_col = jnp.transpose(jnp.broadcast_to(owner_row, (8, rows)))[:, 0:1]
            row_at = lax.broadcasted_iota(jnp.int32, (rows, rows), 0)
            col_at = lax.broadcasted_iota(jnp.int32, (rows, rows), 1)
            earlier = jnp.where((owner_row == owner_col) & (row_at < col_at), 1, 0)
            tgt[...] = owner_row * cap + jnp.sum(earlier, axis=0, keepdims=True)
            conv[...] = jnp.zeros_like(conv)
            tgrad[...] = jnp.zeros_like(tgrad)

        @pl.when(t == 1)
        def _():
            for d in (-1, 1):

                @pl.when(has_f(d))
                def _():
                    aside(d).wait_recv()
                    corner(d).wait_recv()

        @pl.loop(jnp.clip(2 * t - 3, 0, G), jnp.clip(2 * t - 1, 0, G))
        def _(g):
            gather(g)

        done = t - LD

        @pl.when(done >= 0)
        def _():
            for c in twin(done):
                c.wait_recv()
            gathered(done)
            forward(done)

            @pl.when(done < G - 1)
            def _():
                backward(done)

        @pl.when((t >= LS) & (t < LE))
        def _():
            scatter(t - LS, 0, tiles)

    total = regroup(conv[...], lambda p, r: p * LANES + r, lambda p, r: p * width + r, width, F)
    out = ((feat[...].astype(F32) * active[...] + total) * active[...]).astype(BF16)
    sec[...] = out
    far = S // 2

    def skip(d):
        o = (s + d) % S
        return remote(outbox.at[o], recv.at[s], ssend.at[d - 1], srecv.at[d - 1], o, f)

    def boxes(o0):
        slots = lax.broadcasted_iota(jnp.int32, (far * cap, rows), 0) + o0 * cap
        place = jnp.where(slots == tgt[...], 1.0, 0.0).astype(BF16)
        outbox[pl.ds(o0, far)] = jnp.dot(place, out, preferred_element_type=F32).astype(BF16).reshape(far, cap, C)

    half_s = s // far
    boxes((1 - half_s) * far)
    for d in sorted(range(1, S), key=lambda d: abs(d - far)):

        @pl.when((s + d) % S // far != half_s)
        def _():
            skip(d).start()

    boxes(half_s * far)
    for d in range(1, S):

        @pl.when((s + d) % S // far == half_s)
        def _():
            skip(d).start()

    keep = pltpu.make_async_copy(outbox.at[s], recv.at[s], keep_sem)
    keep.start()
    sec_copy = pltpu.make_async_copy(sec, sec_out, out_sem.at[0])
    sec_copy.start()
    backward(G - 1)

    def grad_aside(df):
        n = SIDES.index(df) - 1
        return remote(gsend.at[n], grecv.at[n], bsend.at[n], brecv.at[n], s, f + df)

    def grad_along(ds):
        n = SIDES.index(ds) - 1
        return remote(mids.at[n], back_in.at[n], bsend.at[n + 2], brecv.at[n + 2], s + ds, f)

    half = tiles // 2

    @pl.loop(LE - LS, G)
    def _(g):
        scatter(g, half, tiles - half)

    for d in (-1, 1):
        n = SIDES.index(d) - 1
        for i in range(3):
            at = (half + 3 * n + i) * BLK
            gsend[n, i] = tgrad[:, at : at + BLK].astype(BF16)

        @pl.when(has_f(d))
        def _():
            grad_aside(d).start()


    @pl.loop(LE - LS, G)
    def _(g):
        scatter(g, NB + 1, half - NB - 1)

    for d in (-1, 1):

        @pl.when(has_f(-d))
        def _():
            grad_aside(d).wait_recv()

    def summed(i):
        at = (NB + i) * BLK
        return tgrad[:, at : at + BLK] + grecv[0, i].astype(F32) + grecv[1, i].astype(F32)

    for d in (-1, 1):
        n = SIDES.index(d) - 1
        mids[n] = summed(1 + n).astype(BF16)

        @pl.when(has_s(d))
        def _():
            grad_along(d).start()

    @pl.loop(LE - LS, G)
    def _(g):
        scatter(g, 0, NB + 1)

    centre = summed(0)
    for d in (-1, 1):

        @pl.when(has_s(-d))
        def _():
            grad_along(d).wait_recv()

    back = centre + back_in[0].astype(F32) + back_in[1].astype(F32)
    outs = []
    for b in range(NB):
        r0 = b * BLK
        act_b = active[r0 : r0 + BLK]
        masked, rscale, normed, pre = norm_parts(feat[r0 : r0 + BLK], act_b, gains)
        ag = jnp.transpose(tgrad[:, r0 : r0 + BLK] + jnp.where(h == b, back, 0.0))
        ng = ag * slope[r0 : r0 + BLK]
        mg = rscale * (ng - normed * jnp.mean(ng * normed, axis=-1, keepdims=True))
        fgrad[r0 : r0 + BLK] = ((og[r0 : r0 + BLK].astype(F32) * act_b + mg) * act_b).astype(BF16)
        c = pltpu.make_async_copy(
            fgrad.at[pl.ds(r0, BLK)], fgrad_out.at[pl.ds(r0, BLK)], out_sem.at[1 + b]
        )
        c.start()
        outs.append(c)

    for d in range(1, S):
        skip(d).wait()
    keep.wait()
    sec_copy.wait()
    for d in (-1, 1):

        @pl.when(has_s(-d))
        def _():
            along(d).wait_send()

        @pl.when(has_f(-d))
        def _():
            aside(d).wait_send()
            corner(d).wait_send()

        @pl.when(has_f(d))
        def _():
            grad_aside(d).wait_send()

        @pl.when(has_s(d))
        def _():
            grad_along(d).wait_send()

    @pl.loop(0, G)
    def _(g):
        for d in range(1, Z):
            first(g, d).wait_send()

        for zz in range(Z):
            for c in spread(g, zz):
                c.wait_send()

        for c in across(g) + twin(g):
            c.wait_send()

    for c in outs:
        c.wait()


def copy_kernel(a, b, c, x, y, w, va, vb, vc, load_sem, store_sem):
    jobs = []
    for n, (src, mid, dst) in enumerate(((c, vc, w), (a, va, x), (b, vb, y))):
        load = pltpu.make_async_copy(src, mid, load_sem.at[n])
        load.start()
        jobs.append((load, pltpu.make_async_copy(mid, dst, store_sem.at[n])))
    for load, store in jobs:
        load.wait()
        store.start()
    for load, store in jobs:
        store.wait()


def shards(mesh, features, channel_gain, conv_weight, kernel_map, counts, halo_list, skip_dest, out_grad):
    S, F = mesh.shape["space"], mesh.shape["fsdp"]
    koff, cin, width = conv_weight.shape
    rows, C = features.shape[2:]
    piece = LANES - width
    fits = F == 4 and S % 2 == 0 and cin % 16 == 0 and width == Q * piece and halo_list.shape[2] == 1
    if not (fits and rows == NB * BLK and 9 % NB == 0 and C == rows == F * width):
        return shards_plain(
            features, channel_gain, conv_weight, kernel_map, counts, halo_list, skip_dest, out_grad
        )
    Z, K4 = S // 2, Q + 1
    G = -(-koff // K4)
    tiles = NB + 9
    cap = max(2, 2 * rows // S)
    owners = skip_dest[0, 0].reshape(1, rows)
    vm = pl.BlockSpec(memory_space=pltpu.VMEM)
    sm = pl.BlockSpec(memory_space=pltpu.SMEM)
    hbm = pl.BlockSpec(memory_space=pl.ANY)
    dma = pltpu.SemaphoreType.DMA
    sec, fgrad, recv = pl.pallas_call(
        functools.partial(section_kernel, (S, F, Z, G, K4)),
        out_shape=(
            jax.ShapeDtypeStruct((rows, C), BF16),
            jax.ShapeDtypeStruct((rows, C), BF16),
            jax.ShapeDtypeStruct((S, cap, C), BF16),
        ),
        in_specs=[sm, sm, hbm, vm, hbm, hbm, hbm, vm],
        out_specs=(hbm, hbm, hbm),
        scratch_shapes=[
            pltpu.VMEM((rows, C), BF16),
            pltpu.VMEM((rows, C), BF16),
            pltpu.VMEM((koff, cin, width), BF16),
            pltpu.VMEM((G * K4, 1, rows), jnp.int32),
            pltpu.VMEM((rows, 1), F32),
            pltpu.VMEM((1, rows), jnp.int32),
            pltpu.VMEM((G, F, Q, Z, 2, cin, LANES), BF16),
            pltpu.VMEM((tiles, C, BLK), BF16),
            pltpu.VMEM((G, K4 * C, rows), BF16),
            pltpu.VMEM((rows, F * LANES), F32),
            pltpu.VMEM((rows, F * LANES), BF16),
            pltpu.VMEM((K4 * C, F * LANES), BF16),
            pltpu.VMEM((C, tiles * BLK), F32),
            pltpu.VMEM((2, 3, C, BLK), BF16),
            pltpu.VMEM((2, 3, C, BLK), BF16),
            pltpu.VMEM((2, C, BLK), BF16),
            pltpu.VMEM((2, C, BLK), BF16),
            pltpu.VMEM((S, cap, C), BF16),
            pltpu.VMEM((rows, C), BF16),
            pltpu.VMEM((rows, C), BF16),
            pltpu.VMEM((rows, C), F32),
            dma((G, 3 * Z + 3)),
            dma((G, 3 * Z + 3)),
            dma((6,)),
            dma((6,)),
            dma((S - 1,)),
            dma((S - 1,)),
            dma((4,)),
            dma((4,)),
            dma((4,)),
            dma,
            dma((1 + NB,)),
        ],
        compiler_params=pltpu.CompilerParams(
            collective_id=0, has_side_effects=True, vmem_limit_bytes=56 * 1024 * 1024
        ),
        name="section",
    )(
        halo_list[0, 0], counts[0, 0], features[0, 0], channel_gain, out_grad[0, 0], conv_weight,
        kernel_map[0, 0][:, None], owners,
    )
    whole = (sec, fgrad, recv)
    sec, fgrad, recv = pl.pallas_call(
        copy_kernel,
        out_shape=tuple(jax.ShapeDtypeStruct(v.shape, v.dtype) for v in whole),
        in_specs=[hbm] * 3,
        out_specs=(hbm,) * 3,
        scratch_shapes=[pltpu.VMEM(v.shape, v.dtype) for v in whole] + [dma((3,)), dma((3,))],
        name="deliver",
    )(*whole)
    return (sec[None, None], fgrad[None, None], recv[None, None])


def solution(mesh):
    return jax.shard_map(
        functools.partial(shards, mesh),
        mesh=mesh,
        in_specs=(
            P("space", "fsdp", None, None),
            P(),
            P(None, "space", "fsdp"),
            P("space", "fsdp", None, None),
            P("space", "fsdp", None),
            P("space", "fsdp", None),
            P("space", "fsdp", None, None),
            P("space", "fsdp", None, None),
        ),
        out_specs=(
            P("space", "fsdp", None, None),
            P("space", "fsdp", None, None),
            P("space", "fsdp", None, None, None),
        ),
        check_vma=False,
    )
```

```python
import functools

import jax
import jax.numpy as jnp
from jax import lax
from jax.experimental import pallas as pl
from jax.experimental.pallas import tpu as pltpu
from jax.sharding import PartitionSpec as P

BLK = 128
KOFF = 27
HB = 1
NB = 3
ROWS = 1536


NORM_EPS = 1e-06


def padded(cells, sides, width):
    for axis, dim in sides:
        count = lax.axis_size(axis)
        ends = count - 1
        head = lax.slice_in_dim(cells, 0, width, axis=dim)
        tail = lax.slice_in_dim(cells, cells.shape[dim] - width, cells.shape[dim], axis=dim)
        cells = jnp.concatenate(
            [
                lax.ppermute(tail, axis, [(i, (i + 1) % count) for i in range(ends)]),
                cells,
                lax.ppermute(head, axis, [((i + 1) % count, i) for i in range(ends)]),
            ],
            axis=dim,
        )
    return cells


def passed_along(x, axis, by):
    count = lax.axis_size(axis)
    pairs = [(i, i + by) for i in range(count) if 0 <= i + by < count]
    return lax.ppermute(x, axis, pairs)


def shards_plain(features, channel_gain, conv_weight, kernel_map, counts, halo_list, skip_dest, out_grad):
    own_rows = features[0, 0]
    rowcount = own_rows.shape[0]
    width = own_rows.shape[1]
    slot_ids = jnp.arange(rowcount, dtype=jnp.int32)
    limits = jnp.repeat(counts[0, 0], BLK)
    active = (slot_ids % BLK < limits).astype(jnp.float32)[:, None]
    masked = own_rows * active.astype(jnp.bfloat16)
    masked_f = masked.astype(jnp.float32)
    rscale = lax.rsqrt(jnp.mean(masked_f * masked_f, axis=-1, keepdims=True) + NORM_EPS)
    normed = masked_f * rscale
    pre_act = normed * channel_gain
    act = jax.nn.silu(pre_act).astype(jnp.bfloat16)
    shared = act.reshape(NB, BLK, width)[halo_list[0, 0]]
    beside_all = padded(shared[None, None], (("space", 0), ("fsdp", 1)), 1)
    lookup = jnp.concatenate(
        [act, beside_all.reshape(9 * HB * BLK, width), jnp.zeros((1, width), jnp.bfloat16)], axis=0
    )
    row_grad = out_grad[0, 0] * active.astype(jnp.bfloat16)
    groups = KOFF // 3
    weight_groups = conv_weight.reshape(groups, 3, conv_weight.shape[1], conv_weight.shape[2])
    map_groups = kernel_map[0, 0].reshape(groups, 3, rowcount)

    def group_step(state, inputs_g):
        running, table_grad = state
        weight_piece, neighbours = inputs_g
        widened = lax.all_gather(weight_piece, "fsdp", axis=2, tiled=True)
        full_weights = lax.all_gather(widened, "space", axis=1, tiled=True)
        picked = lookup[neighbours]
        running = running + jnp.einsum(
            "kvc,kcd->vd", picked, full_weights, preferred_element_type=jnp.float32
        )
        backward = jnp.einsum(
            "vd,kcd->kvc", row_grad, full_weights, preferred_element_type=jnp.float32
        )
        table_grad = table_grad.at[neighbours.reshape(-1)].add(backward.reshape(-1, width))
        return ((running, table_grad), None)

    start = (jnp.zeros((rowcount, width), jnp.float32), jnp.zeros((ROWS + 1, width), jnp.float32))
    (conv_sum, table_grad), _ = lax.scan(group_step, start, (weight_groups, map_groups))
    section_out = ((masked_f + conv_sum) * active).astype(jnp.bfloat16)
    owners = skip_dest[0, 0, :, 0]
    earlier = (owners[None, :] == owners[:, None]) & (slot_ids[None, :] < slot_ids[:, None])
    placing = jnp.sum(earlier.astype(jnp.int32), axis=1)
    space_size = lax.axis_size("space")
    capacity = max(2, 2 * rowcount // space_size)
    outbox = (
        jnp.zeros((space_size * capacity, width), jnp.bfloat16)
        .at[owners * capacity + placing]
        .set(section_out)
    )
    received = lax.all_to_all(
        outbox.reshape(space_size, capacity, width),
        "space",
        split_axis=0,
        concat_axis=0,
        tiled=True,
    )
    halo_grad = table_grad[rowcount : rowcount + 9 * HB * BLK].reshape(3, 3, HB, BLK, width)
    middle = halo_grad[1]
    for direction in (1, -1):
        middle = middle + passed_along(
            halo_grad[1 + direction].astype(jnp.bfloat16), "space", direction
        ).astype(jnp.float32)
    returned = middle[1]
    for direction in (1, -1):
        returned = returned + passed_along(
            middle[1 + direction].astype(jnp.bfloat16), "fsdp", direction
        ).astype(jnp.float32)
    act_grad = table_grad[:rowcount].reshape(NB, BLK, width).at[halo_list[0, 0]].add(returned)
    act_grad = act_grad.reshape(rowcount, width)
    sigmoid_pre = jax.nn.sigmoid(pre_act)
    pre_grad = act_grad * sigmoid_pre * (1.0 + pre_act * (1.0 - sigmoid_pre))
    normed_grad = pre_grad * channel_gain
    masked_grad = rscale * (
        normed_grad - normed * jnp.mean(normed_grad * normed, axis=-1, keepdims=True)
    )
    feature_grad = ((row_grad.astype(jnp.float32) + masked_grad) * active).astype(jnp.bfloat16)
    return (section_out[None, None], feature_grad[None, None], received[None, None])


LANES = 128
Q = 3
MESH = pl.DeviceIdType.MESH
F32 = jnp.float32
BF16 = jnp.bfloat16


def moved(x, shift):
    shift = shift % LANES
    return x if shift == 0 else pltpu.roll(x, shift, 1)


def regroup(x, from_of, to_of, width, pieces):
    lanes = lax.broadcasted_iota(jnp.int32, (x.shape[0], LANES), 1)
    tiles = {}
    for p in range(pieces):
        r = 0
        while r < width:
            src, dst = from_of(p, r), to_of(p, r)
            span = min(width - r, LANES - src % LANES, LANES - dst % LANES)
            at = src // LANES * LANES
            value = moved(x[:, at : at + LANES], dst - src)
            low = dst % LANES
            held = tiles.get(dst // LANES, jnp.zeros_like(value))
            tiles[dst // LANES] = jnp.where((lanes >= low) & (lanes < low + span), value, held)
            r += span
    return jnp.concatenate([tiles[t] for t in range(len(tiles))], axis=1)


def norm_parts(feat, active, gain):
    masked = feat.astype(F32) * active
    rscale = lax.rsqrt(jnp.mean(masked * masked, axis=-1, keepdims=True) + NORM_EPS)
    normed = masked * rscale
    return masked, rscale, normed, normed * gain


NT = (((1,), (1,)), ((), ()))
TN = (((0,), (0,)), ((), ()))
SIDES = (0, -1, 1)


def place_of(ds, df):
    return NB + 3 * SIDES.index(df) + SIDES.index(ds)


def section_kernel(
    dims, h_ref, counts, feat_in, gain, og_in, w_in, maps_in, owners,
    sec_out, fgrad_out, recv,
    feat, og, wraw, nmap, active, tgt, wbuf, table, pb, conv, rgt, wcat, tgrad, gsend, grecv, mids, back_in,
    outbox, sec, fgrad, slope,
    wsend, wrecv, hsend, hrecv, ssend, srecv, bsend, brecv, load_sem, keep_sem, out_sem,
):
    S, F, Z, G, K4 = dims
    Y = 2
    rows, C = feat.shape
    width = C // F
    tiles = table.shape[0]
    span = tiles * BLK
    cap = recv.shape[1]
    koff = maps_in.shape[0]
    s = lax.axis_index("space")
    f = lax.axis_index("fsdp")
    z, y = s // Y, s % Y
    fx = (f + 2) % F
    fp = f + 1 - 2 * (f % 2)
    sy = s + 1 - 2 * y

    loads = [
        pltpu.make_async_copy(src, dst, load_sem.at[n])
        for n, (src, dst) in enumerate(
            [(w_in, wraw), (feat_in, feat), (maps_in, nmap.at[pl.ds(0, koff)]), (og_in, og)]
        )
    ]
    for c in loads:
        c.start()

    barrier = pltpu.get_barrier_semaphore()
    for d in range(1, S):
        pl.semaphore_signal(barrier, inc=1, device_id=((s + d) % S, f), device_id_type=MESH)
    for d in range(1, F):
        pl.semaphore_signal(barrier, inc=1, device_id=(s, (f + d) % F), device_id_type=MESH)

    def remote(src, dst, a, b, ss, ff):
        return pltpu.make_async_remote_copy(
            src_ref=src, dst_ref=dst, send_sem=a, recv_sem=b, device_id=(ss, ff), device_id_type=MESH
        )

    def passed(ref, g, i, ss, ff):
        return remote(ref, ref, wsend.at[g, i], wrecv.at[g, i], ss, ff)

    def first(g, d):
        return passed(wbuf.at[g, f, :, z, y], g, d - 1, ((z + d) % Z) * Y + y, f)

    B0 = Z - 1
    low, high = pl.ds(0, Z // 2), pl.ds(Z // 2, Z - Z // 2)

    def spread(g, zz):
        return [
            passed(wbuf.at[g, f, :, zz, y], g, B0 + zz, sy, f),
            passed(wbuf.at[g, f, :, zz, y], g, B0 + Z + zz, s, fx),
        ]

    def across(g):
        return [
            passed(wbuf.at[g, f, :, low, 1 - y], g, B0 + 2 * Z, s, fx),
            passed(wbuf.at[g, fx, :, high, y], g, B0 + 2 * Z + 1, sy, f),
        ]

    def twin(g):
        return [
            passed(wbuf.at[g, f], g, B0 + 2 * Z + 2, s, fp),
            passed(wbuf.at[g, fx], g, B0 + 2 * Z + 3, s, fp),
        ]

    lane_w = lax.broadcasted_iota(jnp.int32, (wraw.shape[1], LANES), 1)
    piece = LANES - width
    loads[0].wait()

    def pack(g):
        wide = []
        for j in range(K4):
            k = g * K4 + j
            if k < koff:
                v = wraw[k].astype(F32)
                wide.append(jnp.concatenate([v, jnp.zeros((v.shape[0], piece), F32)], axis=1))
            else:
                wide.append(jnp.zeros((wraw.shape[1], LANES), F32))
        for q in range(Q):
            extra = moved(wide[Q], width - q * piece)
            wbuf[g, f, q, z, y] = jnp.where(lane_w < width, wide[q], extra).astype(BF16)

    pack(0)

    pl.semaphore_wait(barrier, S + F - 2)

    LB, LC, LD, LS, LE = 2, 4, 5, 6, 8

    def launch(g):
        for c in spread(g, z):
            c.start()

    for d in range(1, Z):
        first(0, d).start()
    launch(0)

    slot = lax.broadcasted_iota(jnp.int32, (BLK, 1), 0)
    for b in range(NB):
        active[b * BLK : (b + 1) * BLK] = jnp.where(slot < counts[b], 1.0, 0.0)
    gains = gain[...].reshape(1, C)
    loads[1].wait()
    h = h_ref[0]
    share = jnp.zeros((C, BLK), F32)
    for b in range(NB):
        r0 = b * BLK
        masked, rscale, normed, pre = norm_parts(feat[r0 : r0 + BLK], active[r0 : r0 + BLK], gains)
        sig = 1.0 / (1.0 + jnp.exp(-pre))
        slope[r0 : r0 + BLK] = sig * (1.0 + pre * (1.0 - sig)) * gains
        act = jnp.transpose(pre * sig)
        table[b] = act.astype(BF16)
        share = jnp.where(h == b, act, share)
    mine = place_of(0, 0)
    table[mine] = share.astype(BF16)

    def along(ds):
        n = SIDES.index(ds) - 1
        return remote(table.at[mine], table.at[place_of(ds, 0)], hsend.at[n], hrecv.at[n], s - ds, f)

    def aside(df):
        n = SIDES.index(df) + 1
        return remote(
            table.at[pl.ds(mine, 1)], table.at[pl.ds(place_of(0, df), 1)], hsend.at[n], hrecv.at[n], s, f - df
        )

    def corner(df):
        n = SIDES.index(df) + 3
        return remote(
            table.at[pl.ds(mine + 1, 2)], table.at[pl.ds(place_of(0, df) + 1, 2)], hsend.at[n], hrecv.at[n], s, f - df
        )

    def has_s(ds):
        return (s + ds >= 0) & (s + ds < S)

    def has_f(df):
        return (f + df >= 0) & (f + df < F)

    for d in (-1, 1):

        @pl.when(has_s(-d))
        def _():
            along(d).start()

        @pl.when(has_f(-d))
        def _():
            aside(d).start()

        @pl.when(jnp.logical_not(has_s(d)))
        def _():
            table[place_of(d, 0)] = jnp.zeros((C, BLK), BF16)

        @pl.when(jnp.logical_not(has_f(d)))
        def _():
            table[pl.ds(place_of(0, d), 3)] = jnp.zeros((3, C, BLK), BF16)

        @pl.when(jnp.logical_not(has_f(-d)))
        def _():
            grecv[SIDES.index(d) - 1] = jnp.zeros((3, C, BLK), BF16)

        @pl.when(jnp.logical_not(has_s(-d)))
        def _():
            back_in[SIDES.index(d) - 1] = jnp.zeros((C, BLK), BF16)

    for g in range(1, G):
        pack(g)
        for d in range(1, Z):
            first(g, d).start()

    for g in range(1, G):
        launch(g)

    loads[2].wait()
    nmap[koff:] = jnp.full((nmap.shape[0] - koff, 1, rows), span, jnp.int32)
    ids = nmap[...]
    block = ids // BLK
    moves = jnp.zeros_like(ids)
    for n in range(9):
        ds, df = n // 3 - 1, n % 3 - 1
        moves = jnp.where(block == NB + n, (place_of(ds, df) - NB - n) * BLK, moves)
    nmap[...] = ids + moves

    for d in (-1, 1):

        @pl.when(has_s(d))
        def _():
            along(d).wait_recv()

    for d in (-1, 1):

        @pl.when(has_f(-d))
        def _():
            corner(d).start()

    def hot(g, p0, count):
        at = lax.broadcasted_iota(jnp.int32, (count * BLK, rows), 0) + p0 * BLK
        return jnp.concatenate(
            [jnp.where(at == nmap[g * K4 + j], 1.0, 0.0).astype(BF16) for j in range(K4)], axis=1
        )

    def gather(g):
        whole = jnp.concatenate([table[p] for p in range(tiles)], axis=1)
        picked = jnp.dot(whole, hot(g, 0, tiles), preferred_element_type=F32).astype(BF16)
        for j in range(K4):
            pb[g, pl.ds(j * C, C)] = picked[:, j * rows : (j + 1) * rows]

    lane_c = lax.broadcasted_iota(jnp.int32, (C, LANES), 1)

    def gathered(g):
        for p in range(F):
            cols = slice(p * LANES, (p + 1) * LANES)
            last = jnp.zeros((C, LANES), F32)
            for q in range(Q):
                part = wbuf[g, p, q].reshape(C, LANES)
                wcat[q * C : (q + 1) * C, cols] = part
                part = moved(part.astype(F32), q * piece - width)
                last = jnp.where((lane_c >= q * piece) & (lane_c < (q + 1) * piece), part, last)
            wcat[Q * C :, cols] = last.astype(BF16)

    def forward(g):
        conv[...] += lax.dot_general(pb[g], wcat[...], TN, preferred_element_type=F32)

    def backward(g):
        grads = lax.dot_general(rgt[...], wcat[...], NT, preferred_element_type=F32).astype(BF16)
        for j in range(K4):
            pb[g, pl.ds(j * rows, rows)] = grads[:, j * C : (j + 1) * C]

    def scatter(g, p0, count):
        cols = slice(p0 * BLK, (p0 + count) * BLK)
        tgrad[:, cols] += lax.dot_general(pb[g], hot(g, p0, count), (((0,), (1,)), ((), ())), preferred_element_type=F32)

    @pl.loop(0, G + LD)
    def _(t):
        @pl.when(t < G)
        def _():
            for d in range(1, Z):
                first(t, d).wait_recv()
                for c in spread(t, (z - d + Z) % Z):
                    c.start()

        @pl.when((t >= LB) & (t < G + LB))
        def _():
            g = t - LB
            for zz in range(Z // 2):
                spread(g, zz)[0].wait_recv()
            across(g)[0].start()
            for zz in range(Z // 2, Z):
                spread(g, zz)[1].wait_recv()
            across(g)[1].start()

        @pl.when((t >= LC) & (t < G + LC))
        def _():
            g = t - LC
            for zz in range(Z // 2, Z):
                spread(g, zz)[0].wait_recv()
            twin(g)[0].start()
            for zz in range(Z // 2):
                spread(g, zz)[1].wait_recv()
            for c in across(g):
                c.wait_recv()
            twin(g)[1].start()

        @pl.when(t == 0)
        def _():
            loads[3].wait()
            rg = og[...].astype(F32) * active[...]
            rgt[...] = (
                regroup(rg, lambda p, r: p * width + r, lambda p, r: p * LANES + r, width, F)
            ).astype(BF16)
            owner_row = owners[...]
            owner_col = jnp.transpose(jnp.broadcast_to(owner_row, (8, rows)))[:, 0:1]
            row_at = lax.broadcasted_iota(jnp.int32, (rows, rows), 0)
            col_at = lax.broadcasted_iota(jnp.int32, (rows, rows), 1)
            earlier = jnp.where((owner_row == owner_col) & (row_at < col_at), 1, 0)
            tgt[...] = owner_row * cap + jnp.sum(earlier, axis=0, keepdims=True)
            conv[...] = jnp.zeros_like(conv)
            tgrad[...] = jnp.zeros_like(tgrad)

        @pl.when(t == 1)
        def _():
            for d in (-1, 1):

                @pl.when(has_f(d))
                def _():
                    aside(d).wait_recv()
                    corner(d).wait_recv()

        @pl.loop(jnp.clip(2 * t - 3, 0, G), jnp.clip(2 * t - 1, 0, G))
        def _(g):
            gather(g)

        done = t - LD

        @pl.when(done >= 0)
        def _():
            for c in twin(done):
                c.wait_recv()
            gathered(done)
            forward(done)

            @pl.when(done < G - 1)
            def _():
                backward(done)

        @pl.when((t >= LS) & (t < LE))
        def _():
            scatter(t - LS, 0, tiles)

    total = regroup(conv[...], lambda p, r: p * LANES + r, lambda p, r: p * width + r, width, F)
    out = ((feat[...].astype(F32) * active[...] + total) * active[...]).astype(BF16)
    sec[...] = out
    far = S // 2

    def skip(d):
        o = (s + d) % S
        return remote(outbox.at[o], recv.at[s], ssend.at[d - 1], srecv.at[d - 1], o, f)

    def boxes(o0):
        slots = lax.broadcasted_iota(jnp.int32, (far * cap, rows), 0) + o0 * cap
        place = jnp.where(slots == tgt[...], 1.0, 0.0).astype(BF16)
        outbox[pl.ds(o0, far)] = jnp.dot(place, out, preferred_element_type=F32).astype(BF16).reshape(far, cap, C)

    half_s = s // far
    boxes((1 - half_s) * far)
    for d in sorted(range(1, S), key=lambda d: abs(d - far)):

        @pl.when((s + d) % S // far != half_s)
        def _():
            skip(d).start()

    boxes(half_s * far)
    for d in range(1, S):

        @pl.when((s + d) % S // far == half_s)
        def _():
            skip(d).start()

    keep = pltpu.make_async_copy(outbox.at[s], recv.at[s], keep_sem)
    keep.start()
    sec_copy = pltpu.make_async_copy(sec, sec_out, out_sem.at[0])
    sec_copy.start()
    backward(G - 1)

    def grad_aside(df):
        n = SIDES.index(df) - 1
        return remote(gsend.at[n], grecv.at[n], bsend.at[n], brecv.at[n], s, f + df)

    def grad_along(ds):
        n = SIDES.index(ds) - 1
        return remote(mids.at[n], back_in.at[n], bsend.at[n + 2], brecv.at[n + 2], s + ds, f)

    half = tiles // 2

    @pl.loop(LE - LS, G)
    def _(g):
        scatter(g, half, tiles - half)

    for d in (-1, 1):
        n = SIDES.index(d) - 1
        for i in range(3):
            at = (half + 3 * n + i) * BLK
            gsend[n, i] = tgrad[:, at : at + BLK].astype(BF16)

        @pl.when(has_f(d))
        def _():
            grad_aside(d).start()


    @pl.loop(LE - LS, G)
    def _(g):
        scatter(g, NB + 1, half - NB - 1)

    for d in (-1, 1):

        @pl.when(has_f(-d))
        def _():
            grad_aside(d).wait_recv()

    def summed(i):
        at = (NB + i) * BLK
        return tgrad[:, at : at + BLK] + grecv[0, i].astype(F32) + grecv[1, i].astype(F32)

    for d in (-1, 1):
        n = SIDES.index(d) - 1
        mids[n] = summed(1 + n).astype(BF16)

        @pl.when(has_s(d))
        def _():
            grad_along(d).start()

    @pl.loop(LE - LS, G)
    def _(g):
        scatter(g, 0, NB + 1)

    centre = summed(0)
    for d in (-1, 1):

        @pl.when(has_s(-d))
        def _():
            grad_along(d).wait_recv()

    back = centre + back_in[0].astype(F32) + back_in[1].astype(F32)
    outs = []
    for b in range(NB):
        r0 = b * BLK
        act_b = active[r0 : r0 + BLK]
        masked, rscale, normed, pre = norm_parts(feat[r0 : r0 + BLK], act_b, gains)
        ag = jnp.transpose(tgrad[:, r0 : r0 + BLK] + jnp.where(h == b, back, 0.0))
        ng = ag * slope[r0 : r0 + BLK]
        mg = rscale * (ng - normed * jnp.mean(ng * normed, axis=-1, keepdims=True))
        fgrad[r0 : r0 + BLK] = ((og[r0 : r0 + BLK].astype(F32) * act_b + mg) * act_b).astype(BF16)
        c = pltpu.make_async_copy(
            fgrad.at[pl.ds(r0, BLK)], fgrad_out.at[pl.ds(r0, BLK)], out_sem.at[1 + b]
        )
        c.start()
        outs.append(c)

    for d in range(1, S):
        skip(d).wait()
    keep.wait()
    sec_copy.wait()
    for d in (-1, 1):

        @pl.when(has_s(-d))
        def _():
            along(d).wait_send()

        @pl.when(has_f(-d))
        def _():
            aside(d).wait_send()
            corner(d).wait_send()

        @pl.when(has_f(d))
        def _():
            grad_aside(d).wait_send()

        @pl.when(has_s(d))
        def _():
            grad_along(d).wait_send()

    @pl.loop(0, G)
    def _(g):
        for d in range(1, Z):
            first(g, d).wait_send()

        for zz in range(Z):
            for c in spread(g, zz):
                c.wait_send()

        for c in across(g) + twin(g):
            c.wait_send()

    for c in outs:
        c.wait()


def copy_kernel(a, b, c, x, y, w, va, vb, vc, load_sem, store_sem):
    jobs = []
    for n, (src, mid, dst) in enumerate(((c, vc, w), (a, va, x), (b, vb, y))):
        load = pltpu.make_async_copy(src, mid, load_sem.at[n])
        load.start()
        jobs.append((load, pltpu.make_async_copy(mid, dst, store_sem.at[n])))
    for load, store in jobs:
        load.wait()
        store.start()
    for load, store in jobs:
        store.wait()


def shards(mesh, features, channel_gain, conv_weight, kernel_map, counts, halo_list, skip_dest, out_grad):
    S, F = mesh.shape["space"], mesh.shape["fsdp"]
    koff, cin, width = conv_weight.shape
    rows, C = features.shape[2:]
    piece = LANES - width
    fits = F == 4 and S % 2 == 0 and cin % 16 == 0 and width == Q * piece and halo_list.shape[2] == 1
    if not (fits and rows == NB * BLK and 9 % NB == 0 and C == rows == F * width):
        return shards_plain(
            features, channel_gain, conv_weight, kernel_map, counts, halo_list, skip_dest, out_grad
        )
    Z, K4 = S // 2, Q + 1
    G = -(-koff // K4)
    tiles = NB + 9
    cap = max(2, 2 * rows // S)
    owners = skip_dest[0, 0].reshape(1, rows)
    vm = pl.BlockSpec(memory_space=pltpu.VMEM)
    sm = pl.BlockSpec(memory_space=pltpu.SMEM)
    hbm = pl.BlockSpec(memory_space=pl.ANY)
    dma = pltpu.SemaphoreType.DMA
    sec, fgrad, recv = pl.pallas_call(
        functools.partial(section_kernel, (S, F, Z, G, K4)),
        out_shape=(
            jax.ShapeDtypeStruct((rows, C), BF16),
            jax.ShapeDtypeStruct((rows, C), BF16),
            jax.ShapeDtypeStruct((S, cap, C), BF16),
        ),
        in_specs=[sm, sm, hbm, vm, hbm, hbm, hbm, vm],
        out_specs=(hbm, hbm, hbm),
        scratch_shapes=[
            pltpu.VMEM((rows, C), BF16),
            pltpu.VMEM((rows, C), BF16),
            pltpu.VMEM((koff, cin, width), BF16),
            pltpu.VMEM((G * K4, 1, rows), jnp.int32),
            pltpu.VMEM((rows, 1), F32),
            pltpu.VMEM((1, rows), jnp.int32),
            pltpu.VMEM((G, F, Q, Z, 2, cin, LANES), BF16),
            pltpu.VMEM((tiles, C, BLK), BF16),
            pltpu.VMEM((G, K4 * C, rows), BF16),
            pltpu.VMEM((rows, F * LANES), F32),
            pltpu.VMEM((rows, F * LANES), BF16),
            pltpu.VMEM((K4 * C, F * LANES), BF16),
            pltpu.VMEM((C, tiles * BLK), F32),
            pltpu.VMEM((2, 3, C, BLK), BF16),
            pltpu.VMEM((2, 3, C, BLK), BF16),
            pltpu.VMEM((2, C, BLK), BF16),
            pltpu.VMEM((2, C, BLK), BF16),
            pltpu.VMEM((S, cap, C), BF16),
            pltpu.VMEM((rows, C), BF16),
            pltpu.VMEM((rows, C), BF16),
            pltpu.VMEM((rows, C), F32),
            dma((G, 3 * Z + 3)),
            dma((G, 3 * Z + 3)),
            dma((6,)),
            dma((6,)),
            dma((S - 1,)),
            dma((S - 1,)),
            dma((4,)),
            dma((4,)),
            dma((4,)),
            dma,
            dma((1 + NB,)),
        ],
        compiler_params=pltpu.CompilerParams(
            collective_id=0, has_side_effects=True, vmem_limit_bytes=56 * 1024 * 1024
        ),
        name="section",
    )(
        halo_list[0, 0], counts[0, 0], features[0, 0], channel_gain, out_grad[0, 0], conv_weight,
        kernel_map[0, 0][:, None], owners,
    )
    whole = (sec, fgrad, recv)
    sec, fgrad, recv = pl.pallas_call(
        copy_kernel,
        out_shape=tuple(jax.ShapeDtypeStruct(v.shape, v.dtype) for v in whole),
        in_specs=[hbm] * 3,
        out_specs=(hbm,) * 3,
        scratch_shapes=[pltpu.VMEM(v.shape, v.dtype) for v in whole] + [dma((3,)), dma((3,))],
        name="deliver",
    )(*whole)
    return (sec[None, None], fgrad[None, None], recv[None, None])


def solution(mesh):
    return jax.shard_map(
        functools.partial(shards, mesh),
        mesh=mesh,
        in_specs=(
            P("space", "fsdp", None, None),
            P(),
            P(None, "space", "fsdp"),
            P("space", "fsdp", None, None),
            P("space", "fsdp", None),
            P("space", "fsdp", None),
            P("space", "fsdp", None, None),
            P("space", "fsdp", None, None),
        ),
        out_specs=(
            P("space", "fsdp", None, None),
            P("space", "fsdp", None, None),
            P("space", "fsdp", None, None, None),
        ),
        check_vma=False,
    )
```
